256 devices in a mesh: seq: 256 (over z, x, y, core).
Axes of the slice: x: 4, y: 4, z: 8, core: 2. Of those that a mesh axis runs over, the one named last changes fastest.
Arguments:
- queries: bfloat16 [131072, 4096], P('seq'), may hold values from -64 to 64
- keys: bfloat16 [131072, 512], P('seq'), may hold values from -64 to 64
- values: bfloat16 [131072, 512], P('seq'), may hold values from -6 to 6
- sink_logits: float32 [64], replicated, may hold values from 3 to 7
Outputs:
- attended: bfloat16 [131072, 4096], P('seq')
- sink_share: float32 [64], replicated
The draws below stay inside these ranges and needn't reach their ends.
All inputs are finite; a program needn't handle non-finite values.
Results may differ from the reference program's by a relative error of at most 0.0042.
Values may be sent and summed in bfloat16 or wider, within the bound.
A program may use at most 128 MiB of HBM per device.

```python
import jax
import jax.numpy as jnp
from jax import lax

Q_HEADS = 64
KV_HEADS = 8
HEAD_DIM = 64
WINDOW = 128
SINK_TOK = 512
TOKENS = 131072


def paired_draw(key):
    key_query = jax.random.fold_in(key, 101)
    key_keys = jax.random.fold_in(key, 102)
    groups = Q_HEADS // KV_HEADS
    position = jnp.arange(TOKENS, dtype=jnp.float32)
    rising = 0.4 * 5.0 ** (position / TOKENS)
    key_draw = jax.random.normal(key_keys, (TOKENS, KV_HEADS, HEAD_DIM), jnp.float32)
    query_draw = jax.random.normal(key_query, (TOKENS, KV_HEADS, groups, HEAD_DIM), jnp.float32)
    query_draw = query_draw * rising[:, None, None, None]
    query_draw = jnp.clip(query_draw, -64.0, 64.0)
    key_draw = jnp.clip(key_draw, -64.0, 64.0)
    return (query_draw.reshape(TOKENS, Q_HEADS * HEAD_DIM), key_draw.reshape(TOKENS, KV_HEADS * HEAD_DIM))


def draw_queries(key, part):
    return paired_draw(key)[0].astype(jnp.bfloat16)


def draw_keys(key, part):
    return paired_draw(key)[1].astype(jnp.bfloat16)


def block_levels(rng, shape, cuts, low, largest):
    loudness, own = 1.0, jax.random.fold_in(rng, 6)
    for axis_at, parts in cuts:
        steps = jnp.exp(jax.random.uniform(jax.random.fold_in(own, axis_at), (parts,), jnp.float32, low / len(cuts), largest / len(cuts)))
        loudness = loudness * jnp.repeat(steps, shape[axis_at] // parts).reshape([-1 if axis == axis_at else 1 for axis in range(len(shape))])
    return loudness


def gaussian(stream_key, shape, deviation, limit, split=(), held_as=jnp.bfloat16):
    values = deviation * jax.random.normal(stream_key, shape, jnp.float32)
    if split:
        values = values * block_levels(stream_key, shape, split, -0.22, 0.18)
    return jnp.clip(values, -limit, limit).astype(held_as)


def setup_inputs(seed: int = 0) -> dict:
    splits = jax.random.split(jax.random.key(seed), 5)
    return {
        "queries": draw_queries(jax.random.fold_in(splits[4], 71), 0),
        "keys": draw_keys(jax.random.fold_in(splits[4], 71), 0),
        "values": gaussian(splits[2], (TOKENS, KV_HEADS * HEAD_DIM), 1.0, 6.0, ((0, 256),)),
        "sink_logits": jnp.clip(jax.random.uniform(splits[3], (Q_HEADS,), jnp.float32, 3.0, 7.0), 3.0, 7.0),
    }


def reference(queries, keys, values, sink_logits):
    groups = Q_HEADS // KV_HEADS
    score_scale = HEAD_DIM ** -0.5
    tile_count = TOKENS // WINDOW
    query_tiles = queries.reshape(tile_count, WINDOW, KV_HEADS, groups, HEAD_DIM)
    padding = jnp.zeros((WINDOW, KV_HEADS * HEAD_DIM), keys.dtype)
    key_padded = jnp.concatenate([padding, keys], axis=0).reshape(TOKENS + WINDOW, KV_HEADS, HEAD_DIM)
    value_padded = jnp.concatenate([padding, values], axis=0).reshape(TOKENS + WINDOW, KV_HEADS, HEAD_DIM)
    sink_key = keys[:SINK_TOK].reshape(SINK_TOK, KV_HEADS, HEAD_DIM).astype(jnp.float32)
    sink_value = values[:SINK_TOK].reshape(SINK_TOK, KV_HEADS, HEAD_DIM).astype(jnp.float32)
    sink_heads = sink_logits.reshape(KV_HEADS, groups).astype(jnp.float32)

    def one_tile(tile_index):
        query_tile = lax.dynamic_index_in_dim(query_tiles, tile_index, 0, keepdims=False).astype(jnp.float32)
        key_tile = lax.dynamic_slice_in_dim(key_padded, tile_index * WINDOW, 2 * WINDOW, 0).astype(jnp.float32)
        value_tile = lax.dynamic_slice_in_dim(value_padded, tile_index * WINDOW, 2 * WINDOW, 0).astype(jnp.float32)
        key_rows = jnp.concatenate([sink_key, key_tile], axis=0)
        value_rows = jnp.concatenate([sink_value, value_tile], axis=0)
        query_pos = tile_index * WINDOW + jnp.arange(WINDOW, dtype=jnp.int32)
        window_pos = tile_index * WINDOW - WINDOW + jnp.arange(2 * WINDOW, dtype=jnp.int32)
        window_ok = (window_pos[None, :] <= query_pos[:, None]) & (window_pos[None, :] > query_pos[:, None] - WINDOW) & (window_pos[None, :] >= 0)
        sink_pos = jnp.arange(SINK_TOK, dtype=jnp.int32)
        sink_ok = sink_pos[None, :] <= query_pos[:, None] - WINDOW
        allowed = jnp.concatenate([sink_ok, window_ok], axis=1)
        scores = jnp.einsum("tkgd,skd->kgts", query_tile, key_rows) * score_scale
        scores = jnp.where(allowed[None, None], scores, -jnp.inf)
        row_max = jnp.maximum(jnp.max(scores, axis=-1), sink_heads[:, :, None])
        weight = jnp.exp(scores - row_max[..., None])
        sink_weight = jnp.exp(sink_heads[:, :, None] - row_max)
        total = jnp.sum(weight, axis=-1) + sink_weight
        weight_bf = weight.astype(jnp.bfloat16).astype(jnp.float32)
        result = jnp.einsum("kgts,skd->tkgd", weight_bf, value_rows)
        result = result / jnp.transpose(total, (2, 0, 1))[..., None]
        shares = jnp.sum(sink_weight / total, axis=-1)
        return result.astype(jnp.bfloat16).reshape(WINDOW, Q_HEADS * HEAD_DIM), shares

    outputs, tile_shares = lax.map(one_tile, jnp.arange(tile_count, dtype=jnp.int32))
    attended = outputs.reshape(TOKENS, Q_HEADS * HEAD_DIM)
    sink_share = jnp.sum(tile_shares, axis=0).reshape(Q_HEADS) / TOKENS
    return attended, sink_share
```

```python
import functools

import jax
import jax.numpy as jnp
from jax import lax
from jax.experimental import pallas as pl
from jax.experimental.pallas import tpu as pltpu
from jax.sharding import Mesh
from jax.sharding import PartitionSpec as P

HEAD_DIM = 64
WINDOW = 128
SINK_TOK = 512
AXES = ("seq_0", "seq_1", "seq_2", "seq_3")
SIZES = (8, 4, 4, 2)
MESH = pl.DeviceIdType.MESH
F32 = jnp.float32
BF16 = jnp.bfloat16
NEG = -1e30
EXP_SCALE = 1.4426950408889634 / 8.0
PIECE = 32


def where_am_i():
    z, x, y, c = (lax.axis_index(a) for a in AXES)
    return z, x, y, c, ((z * 4 + x) * 4 + y) * 2 + c


def coords(lin):
    return (lin // 32, lax.rem(lin // 8, 4), lax.rem(lin // 2, 4), lax.rem(lin, 2))


def plane_peer(z, x, y, c, step):
    return (z, lax.rem(x + step // 4, 4), lax.rem(y + step % 4, 4), c)


def signal(sem, device):
    pl.semaphore_signal(sem, inc=1, device_id=device, device_id_type=MESH)


def spread_kernel(k_ref, v_ref, kv, edge, s1, r1, s2, r2, s3, r3, s4, r4, se, re, sl):
    z, x, y, c, lin = where_am_i()
    xy = 4 * x + y
    first = lin == 0
    relay = z == 0
    rows = pl.ds(pl.multiple_of(xy * PIECE, PIECE), PIECE)

    def remote(src, dst, send, recv, device):
        return pltpu.make_async_remote_copy(
            src_ref=src, dst_ref=dst, send_sem=send, recv_sem=recv, device_id=device, device_id_type=MESH
        )

    barrier = pltpu.get_barrier_semaphore()
    for step in range(1, 16):
        signal(barrier, plane_peer(z, x, y, c, step))
    signal(barrier, (z, x, y, 1 - c))

    @pl.when(lin > 0)
    def _():
        signal(barrier, coords(lin - 1))

    @pl.when(z > 0)
    def _():
        signal(barrier, (0, x, y, c))

    @pl.when(relay & (lin > 0))
    def _():
        signal(barrier, (0, 0, 0, 0))

    waits = 16 + jnp.where(lin < 255, 1, 0) + jnp.where(relay, 7, 0) + jnp.where(first, 31, 0)
    pl.semaphore_wait(barrier, waits)

    @pl.when(first)
    def _():
        for cc, ref in ((0, k_ref), (1, v_ref)):
            for p in range(16):
                part = pl.ds(p * PIECE, PIECE)
                if cc == 0 and p == 0:
                    pltpu.make_async_copy(ref.at[part], kv.at[cc, part], r1).start()
                else:
                    remote(ref.at[part], kv.at[cc, part], s1, r1, (0, p // 4, p % 4, cc)).start()

    @pl.when(lin < 255)
    def _():
        for cc, ref in ((0, k_ref), (1, v_ref)):
            remote(ref.at[pl.ds(384, 128)], edge.at[cc], se.at[cc], re.at[cc], coords(lin + 1)).start()

    @pl.when(first)
    def _():
        for cc, ref in ((0, k_ref), (1, v_ref)):
            pltpu.make_async_copy(ref.at[pl.ds(0, 128)], edge.at[cc], sl.at[cc]).start()

    @pl.when(relay)
    def _():
        remote(kv.at[c, rows], kv.at[c, rows], s2, r1, (z, x, y, c)).wait_recv()
        for zz in range(1, 8):
            remote(kv.at[c, rows], kv.at[c, rows], s2, r2, (zz, x, y, c)).start()

    @pl.when(z > 0)
    def _():
        remote(kv.at[c, rows], kv.at[c, rows], s2, r2, (z, x, y, c)).wait_recv()

    for step in range(1, 16):
        remote(kv.at[c, rows], kv.at[c, rows], s3, r3, plane_peer(z, x, y, c, step)).start()
    all15 = kv.at[c, pl.ds(0, 15 * PIECE)]
    remote(all15, all15, s3, r3, (z, x, y, c)).wait_recv()
    half = remote(kv.at[c], kv.at[c], s4, r4, (z, x, y, 1 - c))
    half.start()
    half.wait_recv()
    half.wait_send()
    remote(all15, all15, s3, r3, (z, x, y, c)).wait_send()

    @pl.when(relay)
    def _():
        seven = kv.at[c, pl.ds(0, 7 * PIECE)]
        remote(seven, seven, s2, r2, (z, x, y, c)).wait_send()

    @pl.when(first)
    def _():
        many = kv.at[:, pl.ds(0, 496)]
        remote(many, many, s1, r1, (z, x, y, c)).wait_send()
        for cc, ref in ((0, k_ref), (1, v_ref)):
            pltpu.make_async_copy(ref.at[pl.ds(0, 128)], edge.at[cc], sl.at[cc]).wait()

    @pl.when(lin < 255)
    def _():
        for cc, ref in ((0, k_ref), (1, v_ref)):
            remote(ref.at[pl.ds(384, 128)], edge.at[cc], se.at[cc], re.at[cc], coords(lin + 1)).wait_send()

    @pl.when(lin > 0)
    def _():
        for cc, ref in ((0, k_ref), (1, v_ref)):
            remote(ref.at[pl.ds(384, 128)], edge.at[cc], se.at[cc], re.at[cc], coords(lin)).wait_recv()


def spread(keys, values):
    vmem = pl.BlockSpec(memory_space=pltpu.VMEM)
    dma = pltpu.SemaphoreType.DMA
    return pl.pallas_call(
        spread_kernel,
        in_specs=[pl.BlockSpec(memory_space=pl.ANY)] * 2,
        out_specs=[vmem, vmem],
        out_shape=[
            jax.ShapeDtypeStruct((2, SINK_TOK, 512), BF16),
            jax.ShapeDtypeStruct((2, WINDOW, 512), BF16),
        ],
        scratch_shapes=[dma(())] * 8 + [dma((2,))] * 3,
        compiler_params=pltpu.CompilerParams(collective_id=0, has_side_effects=True),
    )(keys, values)


def pad_heads(tile):
    low = lax.broadcasted_iota(jnp.int32, tile.shape, 1) < 64
    wide = tile.astype(F32)
    first = jnp.where(low, wide, 0.0)
    second = jnp.where(low, 0.0, wide)
    turned_first = pltpu.roll(first, 64, 1)
    turned_second = pltpu.roll(second, 64, 1)
    return ((first.astype(BF16), turned_first.astype(BF16)), (turned_second.astype(BF16), second.astype(BF16)))


def attend_kernel(sink_ref, q_hbm, kv_ref, edge_ref, k_ref, v_ref, o_hbm, sh_ref, qb, ob, kp, vp, sq, so):
    _, _, _, _, lin = where_am_i()
    for g in range(8):
        cols = pl.ds(g * 512, 512)
        pltpu.make_async_copy(q_hbm.at[:, cols], qb.at[g], sq.at[g]).start()

    low = lax.broadcasted_iota(jnp.int32, (1, 128), 1) < 64
    row = lax.broadcasted_iota(jnp.int32, (128, 128), 0)
    col = lax.broadcasted_iota(jnp.int32, (128, 128), 1)
    own = col <= row
    ones = (jnp.where(low, 1.0, 0.0).astype(BF16), jnp.where(low, 0.0, 1.0).astype(BF16))
    contract_last = (((1,), (1,)), ((), ()))

    def group(g, special):
        pair_cols = pl.ds(pl.multiple_of((g // 2) * 128, 128), 128)

        def prepare(half):
            for which, dst, ref in ((0, kp, k_ref), (1, vp, v_ref)):
                for start, src in (
                    (0, kv_ref.at[which]),
                    (SINK_TOK, edge_ref.at[which]),
                    (SINK_TOK + WINDOW, ref),
                ):
                    made = pad_heads(src[:, pair_cols])[half]
                    size = made[0].shape[0]
                    dst[0, start : start + size, :] = made[0]
                    dst[1, start : start + size, :] = made[1]

        @pl.when(lax.rem(g, 2) == 0)
        def _():
            prepare(0)

        @pl.when(lax.rem(g, 2) == 1)
        def _():
            prepare(1)

        pltpu.make_async_copy(q_hbm.at[:, pl.ds(0, 512)], qb.at[g], sq.at[g]).wait()

        share = [jnp.zeros((1, 128), F32) for _ in range(4)]
        for b in range(4):
            for p in range(4):
                q = qb[g, b * 128 : (b + 1) * 128, p * 128 : (p + 1) * 128]
                weights, tops = [], []
                for e in range(2):
                    far = lax.dot_general(q, kp[e, :SINK_TOK, :], contract_last, preferred_element_type=F32)
                    near = lax.dot_general(
                        q,
                        kp[e, SINK_TOK + b * 128 : SINK_TOK + b * 128 + 256, :],
                        contract_last,
                        preferred_element_type=F32,
                    )
                    before = near[:, :128]
                    if special:
                        index = lin * 4 + b
                        before = jnp.where(index > 0, before, NEG)
                        far = jnp.concatenate(
                            [
                                jnp.where(
                                    col - row <= 128 * (index - 1 - s), far[:, s * 128 : (s + 1) * 128], NEG
                                )
                                for s in range(4)
                            ],
                            axis=1,
                        )
                    close = jnp.where(own, near[:, 128:], before)
                    top = jnp.maximum(
                        jnp.maximum(
                            jnp.maximum(far[:, 0:128], far[:, 128:256]),
                            jnp.maximum(far[:, 256:384], far[:, 384:512]),
                        ),
                        close,
                    )
                    top = jnp.max(top, axis=1, keepdims=True)
                    top = jnp.maximum(top, sink_ref[g * 8 + 2 * p + e] * 8.0)
                    far_w = jnp.exp2((far - top) * EXP_SCALE).astype(BF16)
                    close_w = jnp.exp2((close - top) * EXP_SCALE)
                    before_w = jnp.where(own, 0.0, close_w).astype(BF16)
                    own_w = jnp.where(own, close_w, 0.0).astype(BF16)
                    weights.append((far_w, jnp.concatenate([before_w, own_w], axis=1)))
                    tops.append(top)
                acc = None
                for e in range(2):
                    one = jnp.broadcast_to(ones[e], (SINK_TOK, 128))
                    far_v = jnp.concatenate([vp[e, :SINK_TOK, :], one], axis=1)
                    near_v = jnp.concatenate(
                        [vp[e, SINK_TOK + b * 128 : SINK_TOK + b * 128 + 256, :], one[:256]], axis=1
                    )
                    part = jnp.dot(weights[e][0], far_v, preferred_element_type=F32)
                    part = part + jnp.dot(weights[e][1], near_v, preferred_element_type=F32)
                    acc = part if acc is None else acc + part
                top = jnp.where(low, tops[0], tops[1])
                sink = jnp.where(low, sink_ref[g * 8 + 2 * p], sink_ref[g * 8 + 2 * p + 1]) * 8.0
                sink_w = jnp.exp2((sink - top) * EXP_SCALE)
                inverse = 1.0 / (acc[:, 128:] + sink_w)
                ob[g, b * 128 : (b + 1) * 128, p * 128 : (p + 1) * 128] = (acc[:, :128] * inverse).astype(BF16)
                share[p] = share[p] + jnp.sum(sink_w * inverse, axis=0, keepdims=True)
        sh_ref[g] = jnp.concatenate(share, axis=0)
        cols = pl.ds(pl.multiple_of(g * 512, 512), 512)
        pltpu.make_async_copy(ob.at[g], o_hbm.at[:, cols], so.at[g]).start()

    @pl.when(lin < 2)
    def _():
        @pl.loop(0, 8)
        def _(g):
            group(g, True)

    @pl.when(lin >= 2)
    def _():
        @pl.loop(0, 8)
        def _(g):
            group(g, False)

    for g in range(8):
        pltpu.make_async_copy(ob.at[g], o_hbm.at[:, pl.ds(g * 512, 512)], so.at[g]).wait()


def attend(sink_logits, queries, kv, edge, keys, values):
    vmem = pl.BlockSpec(memory_space=pltpu.VMEM)
    hbm = pl.BlockSpec(memory_space=pl.ANY)
    return pl.pallas_call(
        attend_kernel,
        in_specs=[pl.BlockSpec(memory_space=pltpu.SMEM), hbm, vmem, vmem, vmem, vmem],
        out_specs=[hbm, vmem],
        out_shape=[
            jax.ShapeDtypeStruct((512, 4096), BF16),
            jax.ShapeDtypeStruct((8, 4, 128), F32),
        ],
        scratch_shapes=[
            pltpu.VMEM((8, 512, 512), BF16),
            pltpu.VMEM((8, 512, 512), BF16),
            pltpu.VMEM((2, 1152, 128), BF16),
            pltpu.VMEM((2, 1152, 128), BF16),
            pltpu.SemaphoreType.DMA((8,)),
            pltpu.SemaphoreType.DMA((8,)),
        ],
        compiler_params=pltpu.CompilerParams(vmem_limit_bytes=48 << 20),
    )(sink_logits, queries, kv, edge, keys, values)


def total_kernel(sh_ref, o_ref, one, two, s1, r1, s2, r2):
    z, x, y, c, lin = where_am_i()
    xy = 4 * x + y
    zc = 2 * z + c
    barrier = pltpu.get_barrier_semaphore()

    def other(step):
        at = lax.rem(zc + step, 16)
        return (at // 2, x, y, lax.rem(at, 2))

    for step in range(1, 16):
        signal(barrier, plane_peer(z, x, y, c, step))
        signal(barrier, other(step))
    row = lax.broadcasted_iota(jnp.int32, (32, 128), 0)
    lane = lax.broadcasted_iota(jnp.int32, (32, 128), 1)
    a = sh_ref[...]
    mine = jnp.sum(
        jnp.where(lane == 2 * row, a, 0.0) + jnp.where(lane == 2 * row + 1, pltpu.roll(a, 64, 1), 0.0),
        axis=0,
        keepdims=True,
    )
    one[xy] = jnp.broadcast_to(mine, (8, 128))
    pl.semaphore_wait(barrier, 30)

    def exchange(buf, at, peer, send, recv):
        for step in range(1, 16):
            pltpu.make_async_remote_copy(
                buf.at[at], buf.at[at], send, recv, device_id=peer(step), device_id_type=MESH
            ).start()
        many = buf.at[pl.ds(0, 15)]
        copy = pltpu.make_async_remote_copy(many, many, send, recv, device_id=(z, x, y, c), device_id_type=MESH)
        copy.wait_recv()
        return copy

    plane = functools.partial(plane_peer, z, x, y, c)
    first = exchange(one, xy, plane, s1, r1)
    two[zc] = jnp.sum(one[...], axis=0)
    second = exchange(two, zc, other, s2, r2)
    o_ref[...] = jnp.sum(two[...], axis=0) * (1.0 / 131072)
    first.wait_send()
    second.wait_send()


def total(shares):
    vmem = pl.BlockSpec(memory_space=pltpu.VMEM)
    dma = pltpu.SemaphoreType.DMA
    return pl.pallas_call(
        total_kernel,
        in_specs=[vmem],
        out_specs=vmem,
        out_shape=jax.ShapeDtypeStruct((8, 128), F32),
        scratch_shapes=[pltpu.VMEM((16, 8, 128), F32)] * 2 + [dma(())] * 4,
        compiler_params=pltpu.CompilerParams(collective_id=1, has_side_effects=True),
    )(shares.reshape(32, 128))


def local(queries, keys, values, sink_logits):
    kv, edge = spread(keys, values)
    attended, shares = attend(sink_logits, queries, kv, edge, keys, values)
    return attended, total(shares)[0, :64]


def solution(mesh):
    torus = Mesh(mesh.devices.reshape(SIZES), AXES)
    rows = P(AXES, None)
    return jax.shard_map(
        local, mesh=torus, in_specs=(rows, rows, rows, P()), out_specs=(rows, P()), check_vma=False
    )
```

```python
import functools

import jax
import jax.numpy as jnp
from jax import lax
from jax.experimental import pallas as pl
from jax.experimental.pallas import tpu as pltpu
from jax.sharding import Mesh
from jax.sharding import PartitionSpec as P

WINDOW = 128
SINK_TOK = 512
AXES = ("seq_0", "seq_1", "seq_2", "seq_3")
SIZES = (8, 4, 4, 2)
MESH = pl.DeviceIdType.MESH
F32 = jnp.float32
BF16 = jnp.bfloat16
NEG = -1e30
LOG2E = 1.4426950408889634
PIECE = 32
LATE = 4
EARLY = 8 - LATE
NT = (((1,), (1,)), ((), ()))


def signal(sem, device):
    pl.semaphore_signal(sem, inc=1, device_id=device, device_id_type=MESH)


def coords(lin):
    return (lin // 32, lax.rem(lin // 8, 4), lax.rem(lin // 2, 4), lax.rem(lin, 2))


def padded_keys(tile):
    low = lax.broadcasted_iota(jnp.int32, tile.shape, 1) < 64
    wide = tile.astype(F32) * (LOG2E / 8.0)
    high_term = wide.astype(BF16).astype(F32)
    low_term = wide - high_term
    out = []
    for half in range(2):
        here, moved = [], []
        for term in (high_term, low_term):
            alone = jnp.where(low, term, 0.0) if half == 0 else jnp.where(low, 0.0, term)
            here.append(alone.astype(BF16))
            moved.append(pltpu.roll(alone, 64, 1).astype(BF16))
        here = jnp.concatenate(here, axis=1)
        moved = jnp.concatenate(moved, axis=1)
        out.append((here, moved) if half == 0 else (moved, here))
    return out


def fold(x, op):
    parts = [x[i : i + 8] for i in range(0, x.shape[0], 8)]
    while len(parts) > 1:
        parts = [op(parts[i], parts[i + 1]) for i in range(0, len(parts), 2)]
    return parts[0]


def across(x, op):
    for shift in (4, 2, 1):
        x = op(x, pltpu.roll(x, shift, 0))
    return x


def tall(x, n):
    return jnp.concatenate([x] * n, axis=0)


def kernel(
    sink_ref, q_hbm, k_hbm, v_hbm, o_ref, total_ref,
    qb, kx, vx, kv, kpw, kps, vtw, vts, ow, mw, lw, sb, tb, pb, rb, late_p, late_r, sh, one, two,
    sq, sk, s1, r1, s2, r2, s3, r3, s4, r4, se, re, s5, r5, s6, r6,
):
    z, x, y, c = (lax.axis_index(a) for a in AXES)
    lin = ((z * 4 + x) * 4 + y) * 2 + c
    xy = 4 * x + y
    zc = 2 * z + c
    first = lin == 0
    relay = z == 0
    me = (z, x, y, c)
    rows = pl.ds(pl.multiple_of(xy * PIECE, PIECE), PIECE)

    def plane(step):
        return (z, lax.rem(x + step // 4, 4), lax.rem(y + step % 4, 4), c)

    def column(step):
        at = lax.rem(zc + step, 16)
        return (at // 2, x, y, lax.rem(at, 2))

    def remote(src, dst, send, recv, device):
        return pltpu.make_async_remote_copy(
            src_ref=src, dst_ref=dst, send_sem=send, recv_sem=recv, device_id=device, device_id_type=MESH
        )

    loads = [
        pltpu.make_async_copy(k_hbm, kx.at[pl.ds(WINDOW, 512)], sk.at[0]),
        pltpu.make_async_copy(v_hbm, vx.at[pl.ds(WINDOW, 512)], sk.at[1]),
    ]
    q_load = pltpu.make_async_copy(q_hbm, qb, sq)
    for copy in loads:
        copy.start()
    q_load.start()

    barrier = pltpu.get_barrier_semaphore()

    @pl.when(relay & (lin > 0))
    def _():
        signal(barrier, (0, 0, 0, 0))

    @pl.when(lin > 0)
    def _():
        signal(barrier, coords(lin - 1))

    for step in range(1, 16):
        signal(barrier, plane(step))
        signal(barrier, column(step))

    pl.semaphore_wait(barrier, 30 + jnp.where(lin < 255, 1, 0) + jnp.where(first, 31, 0))
    for copy in loads:
        copy.wait()

    @pl.when(first)
    def _():
        for p in range(16):
            for cc, ref in ((0, kx), (1, vx)):
                src = ref.at[pl.ds(WINDOW + p * PIECE, PIECE)]
                dst = kv.at[cc, pl.ds(p * PIECE, PIECE)]
                if cc == 0 and p == 0:
                    pltpu.make_async_copy(src, dst, r1).start()
                else:
                    remote(src, dst, s1, r1, (0, p // 4, p % 4, cc)).start()
        for i, ref in enumerate((kx, vx)):
            ref[pl.ds(0, WINDOW), :] = jnp.zeros((WINDOW, 512), BF16)

    @pl.when(lin < 255)
    def _():
        for i, ref in enumerate((kx, vx)):
            remote(ref.at[pl.ds(512, WINDOW)], ref.at[pl.ds(0, WINDOW)], se.at[i], re.at[i], coords(lin + 1)).start()

    def prepare(kp, vt, keys, values, start, size, src):
        for pair in range(4):
            cols = pl.ds(pair * 128, 128)
            made = padded_keys(keys[pl.ds(src, size), cols])
            turned = values[pl.ds(src, size), cols].T.reshape(2, 64, size)
            for half in range(2):
                g = 2 * pair + half
                for e in range(2):
                    kp[g, e, start : start + size, :] = made[half][e]
                vt[g, 0:64, start : start + size] = turned[half]

    vtw[:, 64:80, :] = jnp.ones((8, 16, 640), BF16)
    vts[:, 64:80, :] = jnp.ones((8, 16, 512), BF16)
    prepare(kpw, vtw, kx, vx, WINDOW, 512, WINDOW)

    row = lax.broadcasted_iota(jnp.int32, (128, 512), 0)
    col = lax.rem(lax.broadcasted_iota(jnp.int32, (128, 512), 1), 128)
    own = row <= col
    which = lax.broadcasted_iota(jnp.int32, (8, 512), 1) // 128

    def q_tile(g, b):
        cols = [
            qb[b * 128 : b * 128 + 128, pl.ds(pl.multiple_of(g * 512 + p * 128, 128), 128)] for p in range(4)
        ]
        tile = jnp.concatenate(cols, axis=0)
        return jnp.concatenate([tile, tile], axis=1)

    def sink_row(g, e):
        out = jnp.full((8, 512), sink_ref[g * 8 + e] * LOG2E, F32)
        for p in range(1, 4):
            out = jnp.where(which == p, sink_ref[g * 8 + 2 * p + e] * LOG2E, out)
        return out

    def near_scores(g, b, slot):
        start = b * 128
        both = jnp.concatenate([kpw[g, e, start : start + 256, :] for e in range(2)], axis=0)
        s = lax.dot_general(both, q_tile(g, b), NT, preferred_element_type=F32)
        for e in range(2):
            before = s[e * 256 : e * 256 + 128]
            if b == 0:
                before = jnp.where(first, NEG, before)
            w = jnp.where(own, s[e * 256 + 128 : e * 256 + 256], before)
            sb[slot, e, :128] = w
            tb[slot, e] = fold(w, jnp.maximum)

    def near_weights(g, b, slot):
        for e in range(2):
            sink = sink_row(g, e)
            top = jnp.maximum(across(tb[slot, e], jnp.maximum), sink)
            w = jnp.exp2(sb[slot, e, :128] - tall(top, 16))
            pb[slot, e, :128] = jnp.where(own, 0.0, w).astype(BF16)
            pb[slot, e, 128:256] = jnp.where(own, w, 0.0).astype(BF16)
            mw[g, b, e] = top
            rb[slot, e, 0] = jnp.exp2(sink - top)

    def near_values(g, b, slot):
        for e in range(2):
            o = jnp.dot(vtw[g, :, b * 128 : b * 128 + 256], pb[slot, e, :256], preferred_element_type=F32)
            ow[g, b, e] = o[:64]
            lw[g, b, e] = rb[slot, e, 0] + o[64:72]

    def near_pass(blocks):
        units = [(h, b) for h in range(2) for b in blocks]
        n = len(units)
        near_scores(0, blocks[0], 0)

        @pl.loop(0, 4)
        def _(pair):
            for u, (h, b) in enumerate(units):
                slot = u % 2
                if u + 1 < n:
                    near_scores(2 * pair + units[u + 1][0], units[u + 1][1], 1 - slot)
                else:
                    near_scores(jnp.minimum(2 * pair + 2, 6), blocks[0], 1 - slot)
                if u > 0:
                    near_values(2 * pair + units[u - 1][0], units[u - 1][1], 1 - slot)
                else:
                    near_values(jnp.maximum(2 * pair - 1, 0), units[n - 1][1], 1 - slot)
                near_weights(2 * pair + h, b, slot)

        near_values(7, blocks[-1], 1)

    piece = kv.at[c, rows]

    def spread_plane():
        for step in range(1, 16):
            remote(piece, piece, s3, r3, plane(step)).start()

    q_load.wait()
    pb[...] = jnp.zeros_like(pb)
    rb[...] = jnp.zeros_like(rb)
    near_pass((3, 2))

    @pl.when(relay)
    def _():
        remote(piece, piece, s2, r1, me).wait_recv()
        for zz in range(1, 8):
            remote(piece, piece, s2, r2, (zz, x, y, c)).start()
        spread_plane()

    near_pass((1,))

    @pl.when(z > 0)
    def _():
        remote(piece, piece, s2, r2, me).wait_recv()
        spread_plane()

    @pl.when(lin > 0)
    def _():
        for i, ref in enumerate((kx, vx)):
            remote(ref.at[pl.ds(512, WINDOW)], ref.at[pl.ds(0, WINDOW)], se.at[i], re.at[i], me).wait_recv()

    prepare(kpw, vtw, kx, vx, 0, WINDOW, 0)
    near_pass((0,))

    fifteen = kv.at[c, pl.ds(0, 15 * PIECE)]
    remote(fifteen, fifteen, s3, r3, me).wait_recv()
    half = remote(kv.at[c], kv.at[c], s4, r4, (z, x, y, 1 - c))
    half.start()
    half.wait_recv()
    prepare(kps, vts, kv.at[0], kv.at[1], 0, 512, 0)

    def far_scores(g, b, slot, special):
        both = jnp.concatenate([kps[g, e] for e in range(2)], axis=0)
        s = lax.dot_general(both, q_tile(g, b), NT, preferred_element_type=F32)
        for e in range(2):
            part = s[e * 512 : e * 512 + 512]
            if special:
                index = lin * 4 + b
                part = jnp.concatenate(
                    [
                        jnp.where(row - col <= 128 * (index - 1 - i), part[i * 128 : i * 128 + 128], NEG)
                        for i in range(4)
                    ],
                    axis=0,
                )
            sb[slot, e] = part
            tb[slot, e] = fold(part, jnp.maximum)

    def far_weights(g, b, slot, late):
        for e in range(2):
            old = mw[g, b, e]
            top = jnp.maximum(across(tb[slot, e], jnp.maximum), old)
            scale = jnp.exp2(old - top)
            sink = jnp.exp2(sink_row(g, e) - top)
            dst = late_p.at[(g - EARLY) * 4 + b, e] if late else pb.at[slot, e]
            acc = None
            for r in range(0, 512, 64):
                w = jnp.exp2(sb[slot, e, r : r + 64] - tall(top, 8))
                dst[r : r + 64, :] = w.astype(BF16)
                if late:
                    part = fold(w, jnp.add)
                    acc = part if acc is None else acc + part
            if late:
                inverse = 1.0 / (lw[g, b, e] * scale + across(acc, jnp.add))
                sh[g, e] += sink * inverse
                late_r[(g - EARLY) * 4 + b, e, 0] = scale * inverse
                late_r[(g - EARLY) * 4 + b, e, 1] = inverse
            else:
                rb[slot, e, 0] = scale
                rb[slot, e, 1] = sink

    def put(g, b, outs):
        both = jnp.concatenate(outs, axis=0)
        for p in range(4):
            cols = pl.ds(pl.multiple_of(g * 512 + p * 128, 128), 128)
            o_ref[b * 128 : b * 128 + 128, cols] = both[:, p * 128 : p * 128 + 128].T

    def far_values(g, b, slot, share_at):
        outs = []
        for e in range(2):
            o = jnp.dot(vts[g], pb[slot, e], preferred_element_type=F32)
            scale = rb[slot, e, 0]
            inverse = 1.0 / (lw[g, b, e] * scale + o[64:72])
            sh[share_at, e] += rb[slot, e, 1] * inverse
            outs.append((o[:64] * tall(inverse, 8) + ow[g, b, e] * tall(scale * inverse, 8)).astype(BF16))
        put(g, b, outs)

    def late_values(g, b):
        outs = []
        at = (g - EARLY) * 4 + b
        for e in range(2):
            o = jnp.dot(vts[g, 0:64, :], late_p[at, e], preferred_element_type=F32)
            outs.append((o * tall(late_r[at, e, 1], 8) + ow[g, b, e] * tall(late_r[at, e, 0], 8)).astype(BF16))
        put(g, b, outs)

    sh[...] = jnp.zeros_like(sh)

    def far_pass(special):
        far_scores(0, 0, 0, special)

        @pl.loop(0, EARLY)
        def _(g):
            for b in range(4):
                slot = b % 2
                if b < 3:
                    far_scores(g, b + 1, 1 - slot, special)
                else:
                    far_scores(g + 1, 0, 1 - slot, special)
                if b > 0:
                    far_values(g, b - 1, 1 - slot, g)
                else:
                    far_values(jnp.maximum(g - 1, 0), 3, 1 - slot, jnp.where(g > 0, g - 1, 8))
                far_weights(g, b, slot, False)

        far_values(EARLY - 1, 3, 1, EARLY - 1)

        @pl.loop(EARLY, 8)
        def _(g):
            for b in range(4):
                slot = b % 2
                if b < 3:
                    far_scores(g, b + 1, 1 - slot, special)
                else:
                    far_scores(jnp.minimum(g + 1, 7), 0, 1 - slot, special)
                far_weights(g, b, slot, True)

    @pl.when(lin < 2)
    def _():
        far_pass(True)

    @pl.when(lin >= 2)
    def _():
        far_pass(False)

    lane = lax.broadcasted_iota(jnp.int32, (8, 128), 1)
    mine = jnp.zeros((8, 128), F32)
    for g in range(8):
        for e in range(2):
            for p in range(4):
                part = jnp.sum(sh[g, e, :, p * 128 : p * 128 + 128], axis=1, keepdims=True)
                mine = jnp.where(lane == g * 8 + 2 * p + e, part, mine)
    one[xy] = mine
    for step in range(1, 16):
        remote(one.at[xy], one.at[xy], s5, r5, plane(step)).start()

    @pl.loop(EARLY, EARLY + LATE // 2)
    def _(g):
        for b in range(4):
            late_values(g, b)

    many = one.at[pl.ds(0, 15)]
    remote(many, many, s5, r5, me).wait_recv()
    two[zc] = jnp.sum(one[...], axis=0)
    for step in range(1, 16):
        remote(two.at[zc], two.at[zc], s6, r6, column(step)).start()

    @pl.loop(EARLY + LATE // 2, 8)
    def _(g):
        for b in range(4):
            late_values(g, b)

    lots = two.at[pl.ds(0, 15)]
    remote(lots, lots, s6, r6, me).wait_recv()
    total_ref[...] = jnp.sum(two[...], axis=0) * (1.0 / 131072)

    remote(many, many, s5, r5, me).wait_send()
    remote(lots, lots, s6, r6, me).wait_send()
    half.wait_send()
    remote(fifteen, fifteen, s3, r3, me).wait_send()

    @pl.when(relay)
    def _():
        seven = kv.at[c, pl.ds(0, 7 * PIECE)]
        remote(seven, seven, s2, r2, me).wait_send()

    @pl.when(first)
    def _():
        sent = kv.at[:, pl.ds(0, 496)]
        remote(sent, sent, s1, r1, me).wait_send()

    @pl.when(lin < 255)
    def _():
        for i, ref in enumerate((kx, vx)):
            remote(ref.at[pl.ds(512, WINDOW)], ref.at[pl.ds(0, WINDOW)], se.at[i], re.at[i], me).wait_send()


def local(queries, keys, values, sink_logits):
    vmem = pl.BlockSpec(memory_space=pltpu.VMEM)
    hbm = pl.BlockSpec(memory_space=pl.ANY)
    dma = pltpu.SemaphoreType.DMA
    attended, total = pl.pallas_call(
        kernel,
        in_specs=[pl.BlockSpec(memory_space=pltpu.SMEM), hbm, hbm, hbm],
        out_specs=[vmem, vmem],
        out_shape=[jax.ShapeDtypeStruct((512, 4096), BF16), jax.ShapeDtypeStruct((8, 128), F32)],
        scratch_shapes=[
            pltpu.VMEM((512, 4096), BF16),
            pltpu.VMEM((640, 512), BF16),
            pltpu.VMEM((640, 512), BF16),
            pltpu.VMEM((2, 512, 512), BF16),
            pltpu.VMEM((8, 2, 640, 256), BF16),
            pltpu.VMEM((8, 2, 512, 256), BF16),
            pltpu.VMEM((8, 80, 640), BF16),
            pltpu.VMEM((8, 80, 512), BF16),
            pltpu.VMEM((8, 4, 2, 64, 512), F32),
            pltpu.VMEM((8, 4, 2, 8, 512), F32),
            pltpu.VMEM((8, 4, 2, 8, 512), F32),
            pltpu.VMEM((2, 2, 512, 512), F32),
            pltpu.VMEM((2, 2, 8, 512), F32),
            pltpu.VMEM((2, 2, 512, 512), BF16),
            pltpu.VMEM((2, 2, 2, 8, 512), F32),
            pltpu.VMEM((LATE * 4, 2, 512, 512), BF16),
            pltpu.VMEM((LATE * 4, 2, 2, 8, 512), F32),
            pltpu.VMEM((9, 2, 8, 512), F32),
            pltpu.VMEM((16, 8, 128), F32),
            pltpu.VMEM((16, 8, 128), F32),
            dma(()),
            dma((2,)),
        ]
        + [dma(())] * 8
        + [dma((2,))] * 2
        + [dma(())] * 4,
        compiler_params=pltpu.CompilerParams(
            collective_id=0, has_side_effects=True, vmem_limit_bytes=60 << 20
        ),
    )(sink_logits, queries, keys, values)
    return attended, total[0, :64]


def solution(mesh):
    torus = Mesh(mesh.devices.reshape(SIZES), AXES)
    rows = P(AXES, None)
    return jax.shard_map(
        local, mesh=torus, in_specs=(rows, rows, rows, P()), out_specs=(rows, P()), check_vma=False
    )
```

```python
import functools

import jax
import jax.numpy as jnp
from jax import lax
from jax.experimental import pallas as pl
from jax.experimental.pallas import tpu as pltpu
from jax.sharding import Mesh
from jax.sharding import PartitionSpec as P

WINDOW = 128
SINK_TOK = 512
AXES = ("seq_0", "seq_1", "seq_2", "seq_3")
SIZES = (8, 4, 4, 2)
MESH = pl.DeviceIdType.MESH
F32 = jnp.float32
BF16 = jnp.bfloat16
NEG = -1e30
LOG2E = 1.4426950408889634
PIECE = 32
LATE = 4
EARLY = 8 - LATE
NT = (((1,), (1,)), ((), ()))


def signal(sem, device):
    pl.semaphore_signal(sem, inc=1, device_id=device, device_id_type=MESH)


def coords(lin):
    return (lin // 32, lax.rem(lin // 8, 4), lax.rem(lin // 2, 4), lax.rem(lin, 2))


def padded_keys(tile):
    low = lax.broadcasted_iota(jnp.int32, tile.shape, 1) < 64
    wide = tile.astype(F32) * (LOG2E / 8.0)
    high_term = wide.astype(BF16).astype(F32)
    low_term = wide - high_term
    out = []
    for half in range(2):
        here, moved = [], []
        for term in (high_term, low_term):
            alone = jnp.where(low, term, 0.0) if half == 0 else jnp.where(low, 0.0, term)
            here.append(alone.astype(BF16))
            moved.append(pltpu.roll(alone, 64, 1).astype(BF16))
        here = jnp.concatenate(here, axis=1)
        moved = jnp.concatenate(moved, axis=1)
        out.append((here, moved) if half == 0 else (moved, here))
    return out


def fold(x, op):
    parts = [x[i : i + 8] for i in range(0, x.shape[0], 8)]
    while len(parts) > 1:
        odd = parts[len(parts) // 2 * 2 :]
        parts = [op(parts[i], parts[i + 1]) for i in range(0, len(parts) - 1, 2)] + odd
    return parts[0]


def across(x, op):
    for shift in (4, 2, 1):
        x = op(x, pltpu.roll(x, shift, 0))
    return x


def tall(x, n):
    return jnp.concatenate([x] * n, axis=0)


def kernel(
    sink_ref, q_hbm, k_hbm, v_hbm, o_hbm, total_ref,
    qb, ob, kx, vx, kv, kpw, kps, vtw, vts, ow, mw, lw, sb, tb, pb, rb, late_p, late_r, sh, one, two,
    sq, sk, so, s1, r1, s2, r2, s3, r3, s4, r4, se, re, s5, r5, s6, r6,
):
    z, x, y, c = (lax.axis_index(a) for a in AXES)
    lin = ((z * 4 + x) * 4 + y) * 2 + c
    xy = 4 * x + y
    zc = 2 * z + c
    first = lin == 0
    relay = z == 0
    me = (z, x, y, c)
    rows = pl.ds(pl.multiple_of(xy * PIECE, PIECE), PIECE)
    cols = (pl.ds(0, 256), pl.ds(256, 256))

    def plane(step):
        return (z, lax.rem(x + step // 4, 4), lax.rem(y + step % 4, 4), c)

    def column(step):
        at = lax.rem(zc + step, 16)
        return (at // 2, x, y, lax.rem(at, 2))

    def remote(src, dst, send, recv, device):
        return pltpu.make_async_remote_copy(
            src_ref=src, dst_ref=dst, send_sem=send, recv_sem=recv, device_id=device, device_id_type=MESH
        )

    loads = [
        pltpu.make_async_copy(k_hbm, kx.at[pl.ds(WINDOW, 512)], sk.at[0]),
        pltpu.make_async_copy(v_hbm, vx.at[pl.ds(WINDOW, 512)], sk.at[1]),
    ]
    q_load = pltpu.make_async_copy(q_hbm, qb, sq)
    for copy in loads:
        copy.start()
    q_load.start()

    barrier = pltpu.get_barrier_semaphore()

    @pl.when(relay & (lin > 0))
    def _():
        signal(barrier, (0, 0, 0, 0))

    @pl.when(lin > 0)
    def _():
        signal(barrier, coords(lin - 1))

    for step in range(1, 16):
        signal(barrier, plane(step))
        signal(barrier, column(step))

    pl.semaphore_wait(barrier, 30 + jnp.where(lin < 255, 1, 0) + jnp.where(first, 31, 0))
    for copy in loads:
        copy.wait()

    @pl.when(first)
    def _():
        for h in range(2):
            for p in range(16):
                for cc, ref in ((0, kx), (1, vx)):
                    src = ref.at[pl.ds(WINDOW + p * PIECE, PIECE), cols[h]]
                    dst = kv.at[cc, pl.ds(p * PIECE, PIECE), cols[h]]
                    if cc == 0 and p == 0:
                        pltpu.make_async_copy(src, dst, r1.at[h]).start()
                    else:
                        remote(src, dst, s1.at[h], r1.at[h], (0, p // 4, p % 4, cc)).start()
        for i, ref in enumerate((kx, vx)):
            ref[pl.ds(0, WINDOW), :] = jnp.zeros((WINDOW, 512), BF16)

    @pl.when(lin < 255)
    def _():
        for i, ref in enumerate((kx, vx)):
            remote(ref.at[pl.ds(512, WINDOW)], ref.at[pl.ds(0, WINDOW)], se.at[i], re.at[i], coords(lin + 1)).start()

    def prepare(kp, vt, keys, values, start, size, src, pairs=range(4)):
        for pair in pairs:
            lanes = pl.ds(pair * 128, 128)
            made = padded_keys(keys[pl.ds(src, size), lanes])
            turned = values[pl.ds(src, size), lanes].T.reshape(2, 64, size)
            for half in range(2):
                g = 2 * pair + half
                for e in range(2):
                    kp[g, e, start : start + size, :] = made[half][e]
                vt[g, 0:64, start : start + size] = turned[half]

    vtw[:, 64:80, :] = jnp.ones((8, 16, 640), BF16)
    vts[:, 64:80, :] = jnp.ones((8, 16, 512), BF16)
    prepare(kpw, vtw, kx, vx, WINDOW, 512, WINDOW)

    row = lax.broadcasted_iota(jnp.int32, (128, 512), 0)
    col = lax.rem(lax.broadcasted_iota(jnp.int32, (128, 512), 1), 128)
    own = row <= col
    which = lax.broadcasted_iota(jnp.int32, (8, 512), 1) // 128

    def q_tile(g, b):
        cols = [
            qb[b * 128 : b * 128 + 128, pl.ds(pl.multiple_of(g * 512 + p * 128, 128), 128)] for p in range(4)
        ]
        tile = jnp.concatenate(cols, axis=0)
        return jnp.concatenate([tile, tile], axis=1)

    def sink_row(g, e):
        out = jnp.full((8, 512), sink_ref[g * 8 + e] * LOG2E, F32)
        for p in range(1, 4):
            out = jnp.where(which == p, sink_ref[g * 8 + 2 * p + e] * LOG2E, out)
        return out

    def near_scores(g, b, slot):
        start = b * 128
        both = jnp.concatenate([kpw[g, e, start : start + 256, :] for e in range(2)], axis=0)
        s = lax.dot_general(both, q_tile(g, b), NT, preferred_element_type=F32)
        for e in range(2):
            before = s[e * 256 : e * 256 + 128]
            if b == 0:
                before = jnp.where(first, NEG, before)
            w = jnp.where(own, s[e * 256 + 128 : e * 256 + 256], before)
            sb[slot, e, :128] = w
            tb[slot, e] = fold(w, jnp.maximum)

    def near_weights(g, b, slot):
        for e in range(2):
            sink = sink_row(g, e)
            top = jnp.maximum(across(tb[slot, e], jnp.maximum), sink)
            w = jnp.exp2(sb[slot, e, :128] - tall(top, 16))
            pb[slot, e, :128] = jnp.where(own, 0.0, w).astype(BF16)
            pb[slot, e, 128:256] = jnp.where(own, w, 0.0).astype(BF16)
            mw[g, b, e] = top
            rb[slot, e, 0] = jnp.exp2(sink - top)

    def near_values(g, b, slot):
        for e in range(2):
            o = jnp.dot(vtw[g, :, b * 128 : b * 128 + 256], pb[slot, e, :256], preferred_element_type=F32)
            ow[g, b, e] = o[:64]
            lw[g, b, e] = rb[slot, e, 0] + o[64:72]

    def near_pass(blocks):
        units = [(h, b) for h in range(2) for b in blocks]
        n = len(units)
        near_scores(0, blocks[0], 0)

        @pl.loop(0, 4)
        def _(pair):
            for u, (h, b) in enumerate(units):
                slot = u % 2
                if u + 1 < n:
                    near_scores(2 * pair + units[u + 1][0], units[u + 1][1], 1 - slot)
                else:
                    near_scores(jnp.minimum(2 * pair + 2, 6), blocks[0], 1 - slot)
                if u > 0:
                    near_values(2 * pair + units[u - 1][0], units[u - 1][1], 1 - slot)
                else:
                    near_values(jnp.maximum(2 * pair - 1, 0), units[n - 1][1], 1 - slot)
                near_weights(2 * pair + h, b, slot)

        near_values(7, blocks[-1], 1)

    piece = [kv.at[c, rows, cols[h]] for h in range(2)]

    def spread_plane(h):
        for step in range(1, 16):
            remote(piece[h], piece[h], s3.at[h], r3.at[h], plane(step)).start()

    q_load.wait()
    pb[...] = jnp.zeros_like(pb)
    rb[...] = jnp.zeros_like(rb)
    near_pass((3, 2))

    @pl.when(relay)
    def _():
        for h in range(2):
            remote(piece[h], piece[h], s2.at[h], r1.at[h], me).wait_recv()
            for zz in range(1, 8):
                remote(piece[h], piece[h], s2.at[h], r2.at[h], (zz, x, y, c)).start()
            spread_plane(h)

    near_pass((1,))

    @pl.when(z > 0)
    def _():
        remote(piece[0], piece[0], s2.at[0], r2.at[0], me).wait_recv()
        spread_plane(0)

    @pl.when(lin > 0)
    def _():
        for i, ref in enumerate((kx, vx)):
            remote(ref.at[pl.ds(512, WINDOW)], ref.at[pl.ds(0, WINDOW)], se.at[i], re.at[i], me).wait_recv()

    prepare(kpw, vtw, kx, vx, 0, WINDOW, 0)
    near_pass((0,))

    @pl.when(z > 0)
    def _():
        remote(piece[1], piece[1], s2.at[1], r2.at[1], me).wait_recv()
        spread_plane(1)

    fifteen = [kv.at[c, pl.ds(0, 15 * PIECE), cols[h]] for h in range(2)]
    to_sibling = [
        remote(kv.at[c, :, cols[h]], kv.at[c, :, cols[h]], s4.at[h], r4.at[h], (z, x, y, 1 - c)) for h in range(2)
    ]

    def gathered(h):
        remote(fifteen[h], fifteen[h], s3.at[h], r3.at[h], me).wait_recv()
        to_sibling[h].start()

    def arrived(h):
        to_sibling[h].wait_recv()
        prepare(kps, vts, kv.at[0], kv.at[1], 0, 512, 0, (2 * h, 2 * h + 1))

    gathered(0)
    arrived(0)

    def seen(b, kind):
        if kind == 0:
            return b, b > 0
        return 4, kind == 1 and b == 0

    def far_scores(g, b, slot, kind):
        tiles, diagonal = seen(b, kind)
        if tiles == 0:
            return
        n = tiles * 128
        both = jnp.concatenate([kps[g, e, :n] for e in range(2)], axis=0)
        s = lax.dot_general(both, q_tile(g, b), NT, preferred_element_type=F32)
        for e in range(2):
            part = s[e * n : e * n + n]
            if diagonal:
                last = jnp.where(own, part[n - 128 :], NEG)
                part = last if tiles == 1 else jnp.concatenate([part[: n - 128], last], axis=0)
            sb[slot, e, :n] = part
            tb[slot, e] = fold(part, jnp.maximum)

    def far_weights(g, b, slot, kind, late):
        tiles, _ = seen(b, kind)
        n = tiles * 128
        for e in range(2):
            old = mw[g, b, e]
            top = jnp.maximum(across(tb[slot, e], jnp.maximum), old) if tiles else old
            scale = jnp.exp2(old - top)
            sink = jnp.exp2(sink_row(g, e) - top)
            dst = late_p.at[(g - EARLY) * 4 + b, e] if late else pb.at[slot, e]
            acc = jnp.zeros((8, 512), F32)
            for r in range(0, n, 64):
                w = jnp.exp2(sb[slot, e, r : r + 64] - tall(top, 8))
                dst[r : r + 64, :] = w.astype(BF16)
                if late:
                    acc = acc + fold(w, jnp.add)
            if late:
                if n < 512:
                    dst[n:512, :] = jnp.zeros((512 - n, 512), BF16)
                inverse = 1.0 / (lw[g, b, e] * scale + across(acc, jnp.add))
                sh[g, e] += sink * inverse
                late_r[(g - EARLY) * 4 + b, e, 0] = scale * inverse
                late_r[(g - EARLY) * 4 + b, e, 1] = inverse
            else:
                rb[slot, e, 0] = scale
                rb[slot, e, 1] = sink

    def put(g, b, outs):
        both = jnp.concatenate(outs, axis=0)
        for p in range(4):
            lanes = pl.ds(pl.multiple_of(g * 512 + p * 128, 128), 128)
            ob[b * 128 : b * 128 + 128, lanes] = both[:, p * 128 : p * 128 + 128].T

    def far_values(g, b, slot, share_at, kind):
        outs = []
        n = seen(b, kind)[0] * 128
        for e in range(2):
            if n:
                o = jnp.dot(vts[g, :, :n], pb[slot, e, :n], preferred_element_type=F32)
            else:
                o = jnp.zeros((80, 512), F32)
            scale = rb[slot, e, 0]
            inverse = 1.0 / (lw[g, b, e] * scale + o[64:72])
            sh[share_at, e] += rb[slot, e, 1] * inverse
            outs.append((o[:64] * tall(inverse, 8) + ow[g, b, e] * tall(scale * inverse, 8)).astype(BF16))
        put(g, b, outs)

    def late_values(g, b):
        outs = []
        at = (g - EARLY) * 4 + b
        for e in range(2):
            o = jnp.dot(vts[g, 0:64, :], late_p[at, e], preferred_element_type=F32)
            outs.append((o * tall(late_r[at, e, 1], 8) + ow[g, b, e] * tall(late_r[at, e, 0], 8)).astype(BF16))
        put(g, b, outs)

    sh[...] = jnp.zeros_like(sh)
    spans = (pl.ds(0, 2048), pl.ds(2048, 1024), pl.ds(3072, 1024))
    stores = [pltpu.make_async_copy(ob.at[:, spans[i]], o_hbm.at[:, spans[i]], so.at[i]) for i in range(3)]

    def store(i):
        stores[i].start()


    def far_pass(kind):
        far_scores(0, 0, 0, kind)

        @pl.loop(0, EARLY)
        def _(g):
            @pl.when(g == 1)
            def _():
                gathered(1)

            for b in range(4):
                slot = b % 2
                if b < 3:
                    far_scores(g, b + 1, 1 - slot, kind)
                else:
                    far_scores(jnp.minimum(g + 1, EARLY - 1), 0, 1 - slot, kind)
                if b > 0:
                    far_values(g, b - 1, 1 - slot, g, kind)
                else:
                    far_values(jnp.maximum(g - 1, 0), 3, 1 - slot, jnp.where(g > 0, g - 1, 8), kind)
                far_weights(g, b, slot, kind, False)

        far_values(EARLY - 1, 3, 1, EARLY - 1, kind)
        store(0)
        arrived(1)
        far_scores(EARLY, 0, 0, kind)

        @pl.loop(EARLY, 8)
        def _(g):
            for b in range(4):
                slot = b % 2
                if b < 3:
                    far_scores(g, b + 1, 1 - slot, kind)
                else:
                    far_scores(jnp.minimum(g + 1, 7), 0, 1 - slot, kind)
                far_weights(g, b, slot, kind, True)

    @pl.when(lin == 0)
    def _():
        far_pass(0)

    @pl.when(lin == 1)
    def _():
        far_pass(1)

    @pl.when(lin >= 2)
    def _():
        far_pass(2)

    lane = lax.broadcasted_iota(jnp.int32, (8, 128), 1)
    mine = jnp.zeros((8, 128), F32)
    for g in range(8):
        for e in range(2):
            for p in range(4):
                part = jnp.sum(sh[g, e, :, p * 128 : p * 128 + 128], axis=1, keepdims=True)
                mine = jnp.where(lane == g * 8 + 2 * p + e, part, mine)
    one[xy] = mine
    for step in range(1, 16):
        remote(one.at[xy], one.at[xy], s5, r5, plane(step)).start()

    @pl.loop(EARLY, EARLY + LATE // 2)
    def _(g):
        for b in range(4):
            late_values(g, b)

    store(1)
    many = one.at[pl.ds(0, 15)]
    remote(many, many, s5, r5, me).wait_recv()
    two[zc] = jnp.sum(one[...], axis=0)
    for step in range(1, 16):
        remote(two.at[zc], two.at[zc], s6, r6, column(step)).start()

    @pl.loop(EARLY + LATE // 2, 8)
    def _(g):
        for b in range(4):
            late_values(g, b)

    store(2)
    lots = two.at[pl.ds(0, 15)]
    remote(lots, lots, s6, r6, me).wait_recv()
    total_ref[...] = jnp.sum(two[...], axis=0) * (1.0 / 131072)

    remote(many, many, s5, r5, me).wait_send()
    remote(lots, lots, s6, r6, me).wait_send()
    for h in range(2):
        to_sibling[h].wait_send()
        remote(fifteen[h], fifteen[h], s3.at[h], r3.at[h], me).wait_send()

        @pl.when(relay)
        def _():
            seven = kv.at[c, pl.ds(0, 7 * PIECE), cols[h]]
            remote(seven, seven, s2.at[h], r2.at[h], me).wait_send()

        @pl.when(first)
        def _():
            sent = kv.at[:, pl.ds(0, 496), cols[h]]
            remote(sent, sent, s1.at[h], r1.at[h], me).wait_send()

    for copy in stores:
        copy.wait()

    @pl.when(lin < 255)
    def _():
        for i, ref in enumerate((kx, vx)):
            remote(ref.at[pl.ds(512, WINDOW)], ref.at[pl.ds(0, WINDOW)], se.at[i], re.at[i], me).wait_send()


def finish_kernel(a_ref, t_ref, o_ref, share_ref, sem):
    copies = [
        pltpu.make_async_copy(a_ref.at[pl.ds(i * 64, 64)], o_ref.at[pl.ds(i * 64, 64)], sem.at[i]) for i in range(8)
    ]
    for copy in copies:
        copy.start()
    share_ref[...] = t_ref[0, 0:64]
    for copy in copies:
        copy.wait()


def local(queries, keys, values, sink_logits):
    vmem = pl.BlockSpec(memory_space=pltpu.VMEM)
    hbm = pl.BlockSpec(memory_space=pl.ANY)
    dma = pltpu.SemaphoreType.DMA
    attended, total = pl.pallas_call(
        kernel,
        in_specs=[pl.BlockSpec(memory_space=pltpu.SMEM), hbm, hbm, hbm],
        out_specs=[hbm, vmem],
        out_shape=[jax.ShapeDtypeStruct((512, 4096), BF16), jax.ShapeDtypeStruct((8, 128), F32)],
        scratch_shapes=[
            pltpu.VMEM((512, 4096), BF16),
            pltpu.VMEM((512, 4096), BF16),
            pltpu.VMEM((640, 512), BF16),
            pltpu.VMEM((640, 512), BF16),
            pltpu.VMEM((2, 512, 512), BF16),
            pltpu.VMEM((8, 2, 640, 256), BF16),
            pltpu.VMEM((8, 2, 512, 256), BF16),
            pltpu.VMEM((8, 80, 640), BF16),
            pltpu.VMEM((8, 80, 512), BF16),
            pltpu.VMEM((8, 4, 2, 64, 512), F32),
            pltpu.VMEM((8, 4, 2, 8, 512), F32),
            pltpu.VMEM((8, 4, 2, 8, 512), F32),
            pltpu.VMEM((2, 2, 512, 512), F32),
            pltpu.VMEM((2, 2, 8, 512), F32),
            pltpu.VMEM((2, 2, 512, 512), BF16),
            pltpu.VMEM((2, 2, 2, 8, 512), F32),
            pltpu.VMEM((LATE * 4, 2, 512, 512), BF16),
            pltpu.VMEM((LATE * 4, 2, 2, 8, 512), F32),
            pltpu.VMEM((9, 2, 8, 512), F32),
            pltpu.VMEM((16, 8, 128), F32),
            pltpu.VMEM((16, 8, 128), F32),
            dma(()),
            dma((2,)),
            dma((3,)),
        ]
        + [dma((2,))] * 8
        + [dma((2,))] * 2
        + [dma(())] * 4,
        compiler_params=pltpu.CompilerParams(
            collective_id=0, has_side_effects=True, vmem_limit_bytes=60 << 20
        ),
    )(sink_logits, queries, keys, values)
    return pl.pallas_call(
        finish_kernel,
        in_specs=[hbm, vmem],
        out_specs=[hbm, vmem],
        out_shape=[jax.ShapeDtypeStruct((512, 4096), BF16), jax.ShapeDtypeStruct((64,), F32)],
        scratch_shapes=[dma((8,))],
    )(attended, total)


def solution(mesh):
    torus = Mesh(mesh.devices.reshape(SIZES), AXES)
    rows = P(AXES, None)
    return jax.shard_map(
        local, mesh=torus, in_specs=(rows, rows, rows, P()), out_specs=(rows, P()), check_vma=False
    )
```

```python
import functools

import jax
import jax.numpy as jnp
from jax import lax
from jax.experimental import pallas as pl
from jax.experimental.pallas import tpu as pltpu
from jax.sharding import Mesh
from jax.sharding import PartitionSpec as P

WINDOW = 128
SINK_TOK = 512
AXES = ("seq_0", "seq_1", "seq_2", "seq_3")
SIZES = (8, 4, 4, 2)
MESH = pl.DeviceIdType.MESH
F32 = jnp.float32
BF16 = jnp.bfloat16
NEG = -1e30
LOG2E = 1.4426950408889634
PIECE = 32
LATE = 4
EARLY = 8 - LATE
NT = (((1,), (1,)), ((), ()))


def signal(sem, device):
    pl.semaphore_signal(sem, inc=1, device_id=device, device_id_type=MESH)


def coords(lin):
    return (lin // 32, lax.rem(lin // 8, 4), lax.rem(lin // 2, 4), lax.rem(lin, 2))


def padded_keys(tile):
    low = lax.broadcasted_iota(jnp.int32, tile.shape, 1) < 64
    wide = tile.astype(F32) * (LOG2E / 8.0)
    high_term = wide.astype(BF16).astype(F32)
    low_term = wide - high_term
    out = []
    for half in range(2):
        here, moved = [], []
        for term in (high_term, low_term):
            alone = jnp.where(low, term, 0.0) if half == 0 else jnp.where(low, 0.0, term)
            here.append(alone.astype(BF16))
            moved.append(pltpu.roll(alone, 64, 1).astype(BF16))
        here = jnp.concatenate(here, axis=1)
        moved = jnp.concatenate(moved, axis=1)
        out.append((here, moved) if half == 0 else (moved, here))
    return out


def fold(x, op):
    parts = [x[i : i + 8] for i in range(0, x.shape[0], 8)]
    while len(parts) > 1:
        odd = parts[len(parts) // 2 * 2 :]
        parts = [op(parts[i], parts[i + 1]) for i in range(0, len(parts) - 1, 2)] + odd
    return parts[0]


def across(x, op):
    for shift in (4, 2, 1):
        x = op(x, pltpu.roll(x, shift, 0))
    return x


def tall(x, n):
    return jnp.concatenate([x] * n, axis=0)


def kernel(
    sink_ref, q_hbm, k_hbm, v_hbm, o_hbm, total_ref,
    qb, ob, kx, vx, kv, kpw, kps, vtw, vts, ow, mw, lw, sb, tb, pb, rb, late_p, late_r, sh, one, two,
    sq, sk, so, s1, r1, s2, r2, s3, r3, s4, r4, se, re, s5, r5, s6, r6,
):
    z, x, y, c = (lax.axis_index(a) for a in AXES)
    lin = ((z * 4 + x) * 4 + y) * 2 + c
    xy = 4 * x + y
    zc = 2 * z + c
    first = lin == 0
    relay = z == 0
    me = (z, x, y, c)
    rows = pl.ds(pl.multiple_of(xy * PIECE, PIECE), PIECE)
    cols = (pl.ds(0, 256), pl.ds(256, 256))

    def plane(step):
        return (z, lax.rem(x + step // 4, 4), lax.rem(y + step % 4, 4), c)

    def column(step):
        at = lax.rem(zc + step, 16)
        return (at // 2, x, y, lax.rem(at, 2))

    def remote(src, dst, send, recv, device):
        return pltpu.make_async_remote_copy(
            src_ref=src, dst_ref=dst, send_sem=send, recv_sem=recv, device_id=device, device_id_type=MESH
        )

    loads = [
        pltpu.make_async_copy(k_hbm, kx.at[pl.ds(WINDOW, 512)], sk.at[0]),
        pltpu.make_async_copy(v_hbm, vx.at[pl.ds(WINDOW, 512)], sk.at[1]),
    ]
    q_load = pltpu.make_async_copy(q_hbm, qb, sq)
    for copy in loads:
        copy.start()
    q_load.start()

    barrier = pltpu.get_barrier_semaphore()

    @pl.when(relay & (lin > 0))
    def _():
        signal(barrier, (0, 0, 0, 0))

    @pl.when(lin > 0)
    def _():
        signal(barrier, coords(lin - 1))

    for step in range(1, 16):
        signal(barrier, plane(step))
        signal(barrier, column(step))

    pl.semaphore_wait(barrier, 30 + jnp.where(lin < 255, 1, 0) + jnp.where(first, 31, 0))
    for copy in loads:
        copy.wait()

    @pl.when(first)
    def _():
        for h in range(2):
            for p in range(16):
                for cc, ref in ((0, kx), (1, vx)):
                    src = ref.at[pl.ds(WINDOW + p * PIECE, PIECE), cols[h]]
                    dst = kv.at[cc, pl.ds(p * PIECE, PIECE), cols[h]]
                    if cc == 0 and p == 0:
                        pltpu.make_async_copy(src, dst, r1.at[h]).start()
                    else:
                        remote(src, dst, s1.at[h], r1.at[h], (0, p // 4, p % 4, cc)).start()
        for i, ref in enumerate((kx, vx)):
            ref[pl.ds(0, WINDOW), :] = jnp.zeros((WINDOW, 512), BF16)

    @pl.when(lin < 255)
    def _():
        for i, ref in enumerate((kx, vx)):
            remote(ref.at[pl.ds(512, WINDOW)], ref.at[pl.ds(0, WINDOW)], se.at[i], re.at[i], coords(lin + 1)).start()

    def prepare(kp, vt, keys, values, start, size, src, pairs=range(4)):
        for pair in pairs:
            lanes = pl.ds(pair * 128, 128)
            made = padded_keys(keys[pl.ds(src, size), lanes])
            turned = values[pl.ds(src, size), lanes].T.reshape(2, 64, size)
            for half in range(2):
                g = 2 * pair + half
                for e in range(2):
                    kp[g, e, start : start + size, :] = made[half][e]
                vt[g, 0:64, start : start + size] = turned[half]

    vtw[:, 64:80, :] = jnp.ones((8, 16, 640), BF16)
    vts[:, 64:80, :] = jnp.ones((8, 16, 512), BF16)
    prepare(kpw, vtw, kx, vx, WINDOW, 512, WINDOW)

    row = lax.broadcasted_iota(jnp.int32, (128, 512), 0)
    col = lax.rem(lax.broadcasted_iota(jnp.int32, (128, 512), 1), 128)
    own = row <= col
    which = lax.broadcasted_iota(jnp.int32, (8, 512), 1) // 128

    def q_tile(g, b):
        cols = [
            qb[b * 128 : b * 128 + 128, pl.ds(pl.multiple_of(g * 512 + p * 128, 128), 128)] for p in range(4)
        ]
        tile = jnp.concatenate(cols, axis=0)
        return jnp.concatenate([tile, tile], axis=1)

    def sink_row(g, e):
        out = jnp.full((8, 512), sink_ref[g * 8 + e] * LOG2E, F32)
        for p in range(1, 4):
            out = jnp.where(which == p, sink_ref[g * 8 + 2 * p + e] * LOG2E, out)
        return out

    def near_scores(g, b, slot):
        start = b * 128
        both = jnp.concatenate([kpw[g, e, start : start + 256, :] for e in range(2)], axis=0)
        s = lax.dot_general(both, q_tile(g, b), NT, preferred_element_type=F32)
        for e in range(2):
            before = s[e * 256 : e * 256 + 128]
            if b == 0:
                before = jnp.where(first, NEG, before)
            w = jnp.where(own, s[e * 256 + 128 : e * 256 + 256], before)
            sb[slot, e, :128] = w
            tb[slot, e] = fold(w, jnp.maximum)

    def near_weights(g, b, slot):
        for e in range(2):
            sink = sink_row(g, e)
            top = jnp.maximum(across(tb[slot, e], jnp.maximum), sink)
            w = jnp.exp2(sb[slot, e, :128] - tall(top, 16))
            pb[slot, e, :128] = jnp.where(own, 0.0, w).astype(BF16)
            pb[slot, e, 128:256] = jnp.where(own, w, 0.0).astype(BF16)
            mw[g, b, e] = top
            rb[slot, e, 0] = jnp.exp2(sink - top)

    def near_values(g, b, slot):
        for e in range(2):
            o = jnp.dot(vtw[g, :, b * 128 : b * 128 + 256], pb[slot, e, :256], preferred_element_type=F32)
            ow[g, b, e] = o[:64]
            lw[g, b, e] = rb[slot, e, 0] + o[64:72]

    def near_pass(blocks):
        units = [(h, b) for h in range(2) for b in blocks]
        n = len(units)
        near_scores(0, blocks[0], 0)

        @pl.loop(0, 4)
        def _(pair):
            for u, (h, b) in enumerate(units):
                slot = u % 2
                if u + 1 < n:
                    near_scores(2 * pair + units[u + 1][0], units[u + 1][1], 1 - slot)
                else:
                    near_scores(jnp.minimum(2 * pair + 2, 6), blocks[0], 1 - slot)
                if u > 0:
                    near_values(2 * pair + units[u - 1][0], units[u - 1][1], 1 - slot)
                else:
                    near_values(jnp.maximum(2 * pair - 1, 0), units[n - 1][1], 1 - slot)
                near_weights(2 * pair + h, b, slot)

        near_values(7, blocks[-1], 1)

    piece = [kv.at[c, rows, cols[h]] for h in range(2)]

    def spread_plane(h):
        for step in range(1, 16):
            remote(piece[h], piece[h], s3.at[h], r3.at[h], plane(step)).start()

    q_load.wait()
    pb[...] = jnp.zeros_like(pb)
    rb[...] = jnp.zeros_like(rb)
    near_pass((3, 2))

    @pl.when(relay)
    def _():
        for h in range(2):
            remote(piece[h], piece[h], s2.at[h], r1.at[h], me).wait_recv()
            for zz in range(1, 8):
                remote(piece[h], piece[h], s2.at[h], r2.at[h], (zz, x, y, c)).start()
            spread_plane(h)

    near_pass((1,))

    @pl.when(z > 0)
    def _():
        remote(piece[0], piece[0], s2.at[0], r2.at[0], me).wait_recv()
        spread_plane(0)

    @pl.when(lin > 0)
    def _():
        for i, ref in enumerate((kx, vx)):
            remote(ref.at[pl.ds(512, WINDOW)], ref.at[pl.ds(0, WINDOW)], se.at[i], re.at[i], me).wait_recv()

    prepare(kpw, vtw, kx, vx, 0, WINDOW, 0)
    near_pass((0,))

    @pl.when(z > 0)
    def _():
        remote(piece[1], piece[1], s2.at[1], r2.at[1], me).wait_recv()
        spread_plane(1)

    fifteen = [kv.at[c, pl.ds(0, 15 * PIECE), cols[h]] for h in range(2)]
    to_sibling = [
        remote(kv.at[c, :, cols[h]], kv.at[c, :, cols[h]], s4.at[h], r4.at[h], (z, x, y, 1 - c)) for h in range(2)
    ]

    def gathered(h):
        remote(fifteen[h], fifteen[h], s3.at[h], r3.at[h], me).wait_recv()
        to_sibling[h].start()

    def arrived(h):
        to_sibling[h].wait_recv()
        prepare(kps, vts, kv.at[0], kv.at[1], 0, 512, 0, (2 * h, 2 * h + 1))

    gathered(0)
    arrived(0)

    def seen(b, kind):
        if kind == 0:
            return b, b > 0
        return 4, kind == 1 and b == 0

    def far_scores(g, b, slot, kind):
        tiles, diagonal = seen(b, kind)
        if tiles == 0:
            return
        n = tiles * 128
        both = jnp.concatenate([kps[g, e, :n] for e in range(2)], axis=0)
        s = lax.dot_general(both, q_tile(g, b), NT, preferred_element_type=F32)
        for e in range(2):
            part = s[e * n : e * n + n]
            if diagonal:
                last = jnp.where(own, part[n - 128 :], NEG)
                part = last if tiles == 1 else jnp.concatenate([part[: n - 128], last], axis=0)
            sb[slot, e, :n] = part
            tb[slot, e] = fold(part, jnp.maximum)

    def far_weights(g, b, slot, kind, late):
        tiles, _ = seen(b, kind)
        n = tiles * 128
        for e in range(2):
            old = mw[g, b, e]
            top = jnp.maximum(across(tb[slot, e], jnp.maximum), old) if tiles else old
            scale = jnp.exp2(old - top)
            sink = jnp.exp2(sink_row(g, e) - top)
            dst = late_p.at[(g - EARLY) * 4 + b, e] if late else pb.at[slot, e]
            acc = jnp.zeros((8, 512), F32)
            for r in range(0, n, 64):
                w = jnp.exp2(sb[slot, e, r : r + 64] - tall(top, 8))
                dst[r : r + 64, :] = w.astype(BF16)
                if late:
                    acc = acc + fold(w, jnp.add)
            if late:
                if n < 512:
                    dst[n:512, :] = jnp.zeros((512 - n, 512), BF16)
                inverse = 1.0 / (lw[g, b, e] * scale + across(acc, jnp.add))
                sh[g, e] += sink * inverse
                late_r[(g - EARLY) * 4 + b, e, 0] = scale * inverse
                late_r[(g - EARLY) * 4 + b, e, 1] = inverse
            else:
                rb[slot, e, 0] = scale
                rb[slot, e, 1] = sink

    def put(g, b, outs):
        both = jnp.concatenate(outs, axis=0)
        for p in range(4):
            lanes = pl.ds(pl.multiple_of(g * 512 + p * 128, 128), 128)
            ob[b * 128 : b * 128 + 128, lanes] = both[:, p * 128 : p * 128 + 128].T

    def far_values(g, b, slot, share_at, kind):
        outs = []
        n = seen(b, kind)[0] * 128
        for e in range(2):
            if n:
                o = jnp.dot(vts[g, :, :n], pb[slot, e, :n], preferred_element_type=F32)
            else:
                o = jnp.zeros((80, 512), F32)
            scale = rb[slot, e, 0]
            inverse = 1.0 / (lw[g, b, e] * scale + o[64:72])
            sh[share_at, e] += rb[slot, e, 1] * inverse
            outs.append((o[:64] * tall(inverse, 8) + ow[g, b, e] * tall(scale * inverse, 8)).astype(BF16))
        put(g, b, outs)

    def late_values(g, b):
        outs = []
        at = (g - EARLY) * 4 + b
        for e in range(2):
            o = jnp.dot(vts[g, 0:64, :], late_p[at, e], preferred_element_type=F32)
            outs.append((o * tall(late_r[at, e, 1], 8) + ow[g, b, e] * tall(late_r[at, e, 0], 8)).astype(BF16))
        put(g, b, outs)

    sh[...] = jnp.zeros_like(sh)
    spans = (pl.ds(0, 2048), pl.ds(2048, 1024), pl.ds(3072, 1024))
    stores = [pltpu.make_async_copy(ob.at[:, spans[i]], o_hbm.at[:, spans[i]], so.at[i]) for i in range(3)]

    def store(i):
        stores[i].start()


    def far_pass(kind):
        far_scores(0, 0, 0, kind)

        @pl.loop(0, EARLY)
        def _(g):
            @pl.when(g == 1)
            def _():
                gathered(1)

            for b in range(4):
                slot = b % 2
                if b < 3:
                    far_scores(g, b + 1, 1 - slot, kind)
                else:
                    far_scores(jnp.minimum(g + 1, EARLY - 1), 0, 1 - slot, kind)
                if b > 0:
                    far_values(g, b - 1, 1 - slot, g, kind)
                else:
                    far_values(jnp.maximum(g - 1, 0), 3, 1 - slot, jnp.where(g > 0, g - 1, 8), kind)
                far_weights(g, b, slot, kind, False)

        far_values(EARLY - 1, 3, 1, EARLY - 1, kind)
        store(0)
        arrived(1)
        far_scores(EARLY, 0, 0, kind)

        @pl.loop(EARLY, 8)
        def _(g):
            for b in range(4):
                slot = b % 2
                if b < 3:
                    far_scores(g, b + 1, 1 - slot, kind)
                else:
                    far_scores(jnp.minimum(g + 1, 7), 0, 1 - slot, kind)
                far_weights(g, b, slot, kind, True)

    @pl.when(lin == 0)
    def _():
        far_pass(0)

    @pl.when(lin == 1)
    def _():
        far_pass(1)

    @pl.when(lin >= 2)
    def _():
        far_pass(2)

    lane = lax.broadcasted_iota(jnp.int32, (8, 128), 1)
    mine = jnp.zeros((8, 128), F32)
    for g in range(8):
        for e in range(2):
            for p in range(4):
                part = jnp.sum(sh[g, e, :, p * 128 : p * 128 + 128], axis=1, keepdims=True)
                mine = jnp.where(lane == g * 8 + 2 * p + e, part, mine)
    one[xy] = mine
    for step in range(1, 16):
        remote(one.at[xy], one.at[xy], s5, r5, plane(step)).start()

    @pl.loop(EARLY, EARLY + LATE // 2)
    def _(g):
        for b in range(4):
            late_values(g, b)

    store(1)
    many = one.at[pl.ds(0, 15)]
    remote(many, many, s5, r5, me).wait_recv()
    two[zc] = jnp.sum(one[...], axis=0)
    for step in range(1, 16):
        remote(two.at[zc], two.at[zc], s6, r6, column(step)).start()

    @pl.loop(EARLY + LATE // 2, 8)
    def _(g):
        for b in range(4):
            late_values(g, b)

    store(2)
    lots = two.at[pl.ds(0, 15)]
    remote(lots, lots, s6, r6, me).wait_recv()
    total_ref[...] = jnp.sum(two[...], axis=0) * (1.0 / 131072)

    remote(many, many, s5, r5, me).wait_send()
    remote(lots, lots, s6, r6, me).wait_send()
    for h in range(2):
        to_sibling[h].wait_send()
        remote(fifteen[h], fifteen[h], s3.at[h], r3.at[h], me).wait_send()

        @pl.when(relay)
        def _():
            seven = kv.at[c, pl.ds(0, 7 * PIECE), cols[h]]
            remote(seven, seven, s2.at[h], r2.at[h], me).wait_send()

        @pl.when(first)
        def _():
            sent = kv.at[:, pl.ds(0, 496), cols[h]]
            remote(sent, sent, s1.at[h], r1.at[h], me).wait_send()

    for copy in stores:
        copy.wait()

    @pl.when(lin < 255)
    def _():
        for i, ref in enumerate((kx, vx)):
            remote(ref.at[pl.ds(512, WINDOW)], ref.at[pl.ds(0, WINDOW)], se.at[i], re.at[i], me).wait_send()


def finish_kernel(a_ref, t_ref, o_ref, share_ref, buf, come, go):
    parts = [pl.ds(i * 64, 64) for i in range(8)]
    loads = [pltpu.make_async_copy(a_ref.at[part], buf.at[part], come.at[i]) for i, part in enumerate(parts)]
    stores = [pltpu.make_async_copy(buf.at[part], o_ref.at[part], go.at[i]) for i, part in enumerate(parts)]
    for copy in loads:
        copy.start()
    share_ref[...] = t_ref[0, 0:64]
    for load, store in zip(loads, stores):
        load.wait()
        store.start()
    for copy in stores:
        copy.wait()


def local(queries, keys, values, sink_logits):
    vmem = pl.BlockSpec(memory_space=pltpu.VMEM)
    hbm = pl.BlockSpec(memory_space=pl.ANY)
    dma = pltpu.SemaphoreType.DMA
    attended, total = pl.pallas_call(
        kernel,
        in_specs=[pl.BlockSpec(memory_space=pltpu.SMEM), hbm, hbm, hbm],
        out_specs=[hbm, vmem],
        out_shape=[jax.ShapeDtypeStruct((512, 4096), BF16), jax.ShapeDtypeStruct((8, 128), F32)],
        scratch_shapes=[
            pltpu.VMEM((512, 4096), BF16),
            pltpu.VMEM((512, 4096), BF16),
            pltpu.VMEM((640, 512), BF16),
            pltpu.VMEM((640, 512), BF16),
            pltpu.VMEM((2, 512, 512), BF16),
            pltpu.VMEM((8, 2, 640, 256), BF16),
            pltpu.VMEM((8, 2, 512, 256), BF16),
            pltpu.VMEM((8, 80, 640), BF16),
            pltpu.VMEM((8, 80, 512), BF16),
            pltpu.VMEM((8, 4, 2, 64, 512), F32),
            pltpu.VMEM((8, 4, 2, 8, 512), F32),
            pltpu.VMEM((8, 4, 2, 8, 512), F32),
            pltpu.VMEM((2, 2, 512, 512), F32),
            pltpu.VMEM((2, 2, 8, 512), F32),
            pltpu.VMEM((2, 2, 512, 512), BF16),
            pltpu.VMEM((2, 2, 2, 8, 512), F32),
            pltpu.VMEM((LATE * 4, 2, 512, 512), BF16),
            pltpu.VMEM((LATE * 4, 2, 2, 8, 512), F32),
            pltpu.VMEM((9, 2, 8, 512), F32),
            pltpu.VMEM((16, 8, 128), F32),
            pltpu.VMEM((16, 8, 128), F32),
            dma(()),
            dma((2,)),
            dma((3,)),
        ]
        + [dma((2,))] * 8
        + [dma((2,))] * 2
        + [dma(())] * 4,
        compiler_params=pltpu.CompilerParams(
            collective_id=0, has_side_effects=True, vmem_limit_bytes=60 << 20
        ),
    )(sink_logits, queries, keys, values)
    return pl.pallas_call(
        finish_kernel,
        in_specs=[hbm, vmem],
        out_specs=[hbm, vmem],
        out_shape=[jax.ShapeDtypeStruct((512, 4096), BF16), jax.ShapeDtypeStruct((64,), F32)],
        scratch_shapes=[pltpu.VMEM((512, 4096), BF16), dma((8,)), dma((8,))],
    )(attended, total)


def solution(mesh):
    torus = Mesh(mesh.devices.reshape(SIZES), AXES)
    rows = P(AXES, None)
    return jax.shard_map(
        local, mesh=torus, in_specs=(rows, rows, rows, P()), out_specs=(rows, P()), check_vma=False
    )
```

```python
import functools

import jax
import jax.numpy as jnp
from jax import lax
from jax.experimental import pallas as pl
from jax.experimental.pallas import tpu as pltpu
from jax.sharding import Mesh
from jax.sharding import PartitionSpec as P

WINDOW = 128
SINK_TOK = 512
AXES = ("seq_0", "seq_1", "seq_2", "seq_3")
SIZES = (8, 4, 4, 2)
MESH = pl.DeviceIdType.MESH
F32 = jnp.float32
BF16 = jnp.bfloat16
NEG = -1e30
LOG2E = 1.4426950408889634
PIECE = 32
LATE = 4
EARLY = 8 - LATE
NT = (((1,), (1,)), ((), ()))


def signal(sem, device):
    pl.semaphore_signal(sem, inc=1, device_id=device, device_id_type=MESH)


def coords(lin):
    return (lin // 32, lax.rem(lin // 8, 4), lax.rem(lin // 2, 4), lax.rem(lin, 2))


def padded_keys(tile):
    low = lax.broadcasted_iota(jnp.int32, tile.shape, 1) < 64
    wide = tile.astype(F32) * (LOG2E / 8.0)
    high_term = wide.astype(BF16).astype(F32)
    low_term = wide - high_term
    out = []
    for half in range(2):
        here, moved = [], []
        for term in (high_term, low_term):
            alone = jnp.where(low, term, 0.0) if half == 0 else jnp.where(low, 0.0, term)
            here.append(alone.astype(BF16))
            moved.append(pltpu.roll(alone, 64, 1).astype(BF16))
        here = jnp.concatenate(here, axis=1)
        moved = jnp.concatenate(moved, axis=1)
        out.append((here, moved) if half == 0 else (moved, here))
    return out


def fold(x, op):
    parts = [x[i : i + 8] for i in range(0, x.shape[0], 8)]
    while len(parts) > 1:
        odd = parts[len(parts) // 2 * 2 :]
        parts = [op(parts[i], parts[i + 1]) for i in range(0, len(parts) - 1, 2)] + odd
    return parts[0]


def across(x, op):
    for shift in (4, 2, 1):
        x = op(x, pltpu.roll(x, shift, 0))
    return x


def tall(x, n):
    return jnp.concatenate([x] * n, axis=0)


def kernel(
    sink_ref, q_hbm, k_hbm, v_hbm, o_hbm, total_ref,
    qb, ob, kx, vx, kv, kpw, kps, vtw, vts, ow, mw, lw, sb, tb, pb, rb, late_p, late_r, sh, one, two,
    ready, sq, sk, so, s1, r1, s2, r2, s3, r3, s4, r4, se, re, s5, r5, s6, r6,
):
    z, x, y, c = (lax.axis_index(a) for a in AXES)
    lin = ((z * 4 + x) * 4 + y) * 2 + c
    xy = 4 * x + y
    zc = 2 * z + c
    first = lin == 0
    relay = z == 0
    me = (z, x, y, c)
    rows = pl.ds(pl.multiple_of(xy * PIECE, PIECE), PIECE)
    cols = (pl.ds(0, 256), pl.ds(256, 256))

    def plane(step):
        return (z, lax.rem(x + step // 4, 4), lax.rem(y + step % 4, 4), c)

    def column(step):
        at = lax.rem(zc + step, 16)
        return (at // 2, x, y, lax.rem(at, 2))

    def remote(src, dst, send, recv, device):
        return pltpu.make_async_remote_copy(
            src_ref=src, dst_ref=dst, send_sem=send, recv_sem=recv, device_id=device, device_id_type=MESH
        )

    loads = [
        pltpu.make_async_copy(k_hbm, kx.at[pl.ds(WINDOW, 512)], sk.at[0]),
        pltpu.make_async_copy(v_hbm, vx.at[pl.ds(WINDOW, 512)], sk.at[1]),
    ]
    q_load = pltpu.make_async_copy(q_hbm, qb, sq)
    for copy in loads:
        copy.start()
    q_load.start()

    barrier = pltpu.get_barrier_semaphore()

    @pl.when(relay & (c == 1))
    def _():
        signal(barrier, (0, 0, 0, 0))

    for step in range(1, 16):
        signal(barrier, plane(step))
    signal(barrier, (z, x, y, 1 - c))

    @pl.when((c == 0) & (lin > 0))
    def _():
        signal(barrier, coords(lin - 1))

    @pl.when(relay)
    def _():
        for zz in range(1, 8):
            signal(barrier, (zz, x, y, c))

    from_next = jnp.where((c == 1) & (lin < 255), 1, 0)
    pl.semaphore_wait(barrier, 16 + from_next + jnp.where(first, 16, 0) + jnp.where(relay, 0, 1))

    @pl.when(z > 0)
    def _():
        signal(ready, (0, x, y, c))

    for copy in loads:
        copy.wait()

    @pl.when(first)
    def _():
        for h in range(2):
            for p in range(16):
                for cc, ref in ((0, kx), (1, vx)):
                    src = ref.at[pl.ds(WINDOW + p * PIECE, PIECE), cols[h]]
                    dst = kv.at[cc, pl.ds(p * PIECE, PIECE), cols[h]]
                    if cc == 0 and p == 0:
                        pltpu.make_async_copy(src, dst, r1.at[h]).start()
                    else:
                        remote(src, dst, s1.at[h], r1.at[h], (0, p // 4, p % 4, cc)).start()
        for i, ref in enumerate((kx, vx)):
            ref[pl.ds(0, WINDOW), :] = jnp.zeros((WINDOW, 512), BF16)

    @pl.when(lin < 255)
    def _():
        for i, ref in enumerate((kx, vx)):
            remote(ref.at[pl.ds(512, WINDOW)], ref.at[pl.ds(0, WINDOW)], se.at[i], re.at[i], coords(lin + 1)).start()

    def prepare(kp, vt, keys, values, start, size, src, pairs=range(4)):
        for pair in pairs:
            lanes = pl.ds(pair * 128, 128)
            made = padded_keys(keys[pl.ds(src, size), lanes])
            turned = values[pl.ds(src, size), lanes].T.reshape(2, 64, size)
            for half in range(2):
                g = 2 * pair + half
                for e in range(2):
                    kp[g, e, start : start + size, :] = made[half][e]
                vt[g, 0:64, start : start + size] = turned[half]

    vtw[:, 64:80, :] = jnp.ones((8, 16, 640), BF16)
    vts[:, 64:80, :] = jnp.ones((8, 16, 512), BF16)
    prepare(kpw, vtw, kx, vx, WINDOW, 512, WINDOW)

    row = lax.broadcasted_iota(jnp.int32, (128, 512), 0)
    col = lax.rem(lax.broadcasted_iota(jnp.int32, (128, 512), 1), 128)
    own = row <= col
    which = lax.broadcasted_iota(jnp.int32, (8, 512), 1) // 128

    def q_tile(g, b):
        cols = [
            qb[b * 128 : b * 128 + 128, pl.ds(pl.multiple_of(g * 512 + p * 128, 128), 128)] for p in range(4)
        ]
        tile = jnp.concatenate(cols, axis=0)
        return jnp.concatenate([tile, tile], axis=1)

    def sink_row(g, e):
        out = jnp.full((8, 512), sink_ref[g * 8 + e] * LOG2E, F32)
        for p in range(1, 4):
            out = jnp.where(which == p, sink_ref[g * 8 + 2 * p + e] * LOG2E, out)
        return out

    def near_scores(g, b, slot):
        start = b * 128
        both = jnp.concatenate([kpw[g, e, start : start + 256, :] for e in range(2)], axis=0)
        s = lax.dot_general(both, q_tile(g, b), NT, preferred_element_type=F32)
        for e in range(2):
            before = s[e * 256 : e * 256 + 128]
            if b == 0:
                before = jnp.where(first, NEG, before)
            w = jnp.where(own, s[e * 256 + 128 : e * 256 + 256], before)
            sb[slot, e, :128] = w
            tb[slot, e] = fold(w, jnp.maximum)

    def near_weights(g, b, slot):
        for e in range(2):
            sink = sink_row(g, e)
            top = jnp.maximum(across(tb[slot, e], jnp.maximum), sink)
            w = jnp.exp2(sb[slot, e, :128] - tall(top, 16))
            pb[slot, e, :128] = jnp.where(own, 0.0, w).astype(BF16)
            pb[slot, e, 128:256] = jnp.where(own, w, 0.0).astype(BF16)
            mw[g, b, e] = top
            rb[slot, e, 0] = jnp.exp2(sink - top)

    def near_values(g, b, slot):
        for e in range(2):
            o = jnp.dot(vtw[g, :, b * 128 : b * 128 + 256], pb[slot, e, :256], preferred_element_type=F32)
            ow[g, b, e] = o[:64]
            lw[g, b, e] = rb[slot, e, 0] + o[64:72]

    def near_pass(blocks):
        units = [(h, b) for h in range(2) for b in blocks]
        n = len(units)
        near_scores(0, blocks[0], 0)

        @pl.loop(0, 4)
        def _(pair):
            for u, (h, b) in enumerate(units):
                slot = u % 2
                if u + 1 < n:
                    near_scores(2 * pair + units[u + 1][0], units[u + 1][1], 1 - slot)
                else:
                    near_scores(jnp.minimum(2 * pair + 2, 6), blocks[0], 1 - slot)
                if u > 0:
                    near_values(2 * pair + units[u - 1][0], units[u - 1][1], 1 - slot)
                else:
                    near_values(jnp.maximum(2 * pair - 1, 0), units[n - 1][1], 1 - slot)
                near_weights(2 * pair + h, b, slot)

        near_values(7, blocks[-1], 1)

    piece = [kv.at[c, rows, cols[h]] for h in range(2)]

    def spread_plane(h):
        for step in range(1, 16):
            remote(piece[h], piece[h], s3.at[h], r3.at[h], plane(step)).start()

    q_load.wait()
    pb[...] = jnp.zeros_like(pb)
    rb[...] = jnp.zeros_like(rb)
    near_pass((3, 2))

    @pl.when(relay)
    def _():
        pl.semaphore_wait(ready, 7)
        for h in range(2):
            remote(piece[h], piece[h], s2.at[h], r1.at[h], me).wait_recv()
            for zz in range(1, 8):
                remote(piece[h], piece[h], s2.at[h], r2.at[h], (zz, x, y, c)).start()
            spread_plane(h)

    near_pass((1,))

    @pl.when(z > 0)
    def _():
        remote(piece[0], piece[0], s2.at[0], r2.at[0], me).wait_recv()
        spread_plane(0)

    @pl.when(lin > 0)
    def _():
        for i, ref in enumerate((kx, vx)):
            remote(ref.at[pl.ds(512, WINDOW)], ref.at[pl.ds(0, WINDOW)], se.at[i], re.at[i], me).wait_recv()

    prepare(kpw, vtw, kx, vx, 0, WINDOW, 0)
    near_pass((0,))

    @pl.when(z > 0)
    def _():
        remote(piece[1], piece[1], s2.at[1], r2.at[1], me).wait_recv()
        spread_plane(1)

    fifteen = [kv.at[c, pl.ds(0, 15 * PIECE), cols[h]] for h in range(2)]
    to_sibling = [
        remote(kv.at[c, :, cols[h]], kv.at[c, :, cols[h]], s4.at[h], r4.at[h], (z, x, y, 1 - c)) for h in range(2)
    ]

    def gathered(h):
        remote(fifteen[h], fifteen[h], s3.at[h], r3.at[h], me).wait_recv()
        to_sibling[h].start()

    def arrived(h):
        to_sibling[h].wait_recv()
        prepare(kps, vts, kv.at[0], kv.at[1], 0, 512, 0, (2 * h, 2 * h + 1))

    gathered(0)
    arrived(0)

    def seen(b, kind):
        if kind == 0:
            return b, b > 0
        return 4, kind == 1 and b == 0

    def far_scores(g, b, slot, kind):
        tiles, diagonal = seen(b, kind)
        if tiles == 0:
            return
        n = tiles * 128
        both = jnp.concatenate([kps[g, e, :n] for e in range(2)], axis=0)
        s = lax.dot_general(both, q_tile(g, b), NT, preferred_element_type=F32)
        for e in range(2):
            part = s[e * n : e * n + n]
            if diagonal:
                last = jnp.where(own, part[n - 128 :], NEG)
                part = last if tiles == 1 else jnp.concatenate([part[: n - 128], last], axis=0)
            sb[slot, e, :n] = part
            tb[slot, e] = fold(part, jnp.maximum)

    def far_weights(g, b, slot, kind, late):
        tiles, _ = seen(b, kind)
        n = tiles * 128
        for e in range(2):
            old = mw[g, b, e]
            top = jnp.maximum(across(tb[slot, e], jnp.maximum), old) if tiles else old
            scale = jnp.exp2(old - top)
            sink = jnp.exp2(sink_row(g, e) - top)
            dst = late_p.at[(g - EARLY) * 4 + b, e] if late else pb.at[slot, e]
            acc = jnp.zeros((8, 512), F32)
            for r in range(0, n, 64):
                w = jnp.exp2(sb[slot, e, r : r + 64] - tall(top, 8))
                dst[r : r + 64, :] = w.astype(BF16)
                if late:
                    acc = acc + fold(w, jnp.add)
            if late:
                if n < 512:
                    dst[n:512, :] = jnp.zeros((512 - n, 512), BF16)
                inverse = 1.0 / (lw[g, b, e] * scale + across(acc, jnp.add))
                sh[g, e] += sink * inverse
                late_r[(g - EARLY) * 4 + b, e, 0] = scale * inverse
                late_r[(g - EARLY) * 4 + b, e, 1] = inverse
            else:
                rb[slot, e, 0] = scale
                rb[slot, e, 1] = sink

    def put(g, b, outs):
        both = jnp.concatenate(outs, axis=0)
        for p in range(4):
            lanes = pl.ds(pl.multiple_of(g * 512 + p * 128, 128), 128)
            ob[b * 128 : b * 128 + 128, lanes] = both[:, p * 128 : p * 128 + 128].T

    def far_values(g, b, slot, share_at, kind):
        outs = []
        n = seen(b, kind)[0] * 128
        for e in range(2):
            if n:
                o = jnp.dot(vts[g, :, :n], pb[slot, e, :n], preferred_element_type=F32)
            else:
                o = jnp.zeros((80, 512), F32)
            scale = rb[slot, e, 0]
            inverse = 1.0 / (lw[g, b, e] * scale + o[64:72])
            sh[share_at, e] += rb[slot, e, 1] * inverse
            outs.append((o[:64] * tall(inverse, 8) + ow[g, b, e] * tall(scale * inverse, 8)).astype(BF16))
        put(g, b, outs)

    def late_values(g, b):
        outs = []
        at = (g - EARLY) * 4 + b
        for e in range(2):
            o = jnp.dot(vts[g, 0:64, :], late_p[at, e], preferred_element_type=F32)
            outs.append((o * tall(late_r[at, e, 1], 8) + ow[g, b, e] * tall(late_r[at, e, 0], 8)).astype(BF16))
        put(g, b, outs)

    sh[...] = jnp.zeros_like(sh)
    spans = (pl.ds(0, 2048), pl.ds(2048, 1024), pl.ds(3072, 1024))
    stores = [pltpu.make_async_copy(ob.at[:, spans[i]], o_hbm.at[:, spans[i]], so.at[i]) for i in range(3)]

    def store(i):
        stores[i].start()


    def far_pass(kind):
        far_scores(0, 0, 0, kind)

        @pl.loop(0, EARLY)
        def _(g):
            @pl.when(g == 1)
            def _():
                gathered(1)

            for b in range(4):
                slot = b % 2
                if b < 3:
                    far_scores(g, b + 1, 1 - slot, kind)
                else:
                    far_scores(jnp.minimum(g + 1, EARLY - 1), 0, 1 - slot, kind)
                if b > 0:
                    far_values(g, b - 1, 1 - slot, g, kind)
                else:
                    far_values(jnp.maximum(g - 1, 0), 3, 1 - slot, jnp.where(g > 0, g - 1, 8), kind)
                far_weights(g, b, slot, kind, False)

        far_values(EARLY - 1, 3, 1, EARLY - 1, kind)
        store(0)
        arrived(1)
        far_scores(EARLY, 0, 0, kind)

        @pl.loop(EARLY, 8)
        def _(g):
            for b in range(4):
                slot = b % 2
                if b < 3:
                    far_scores(g, b + 1, 1 - slot, kind)
                else:
                    far_scores(jnp.minimum(g + 1, 7), 0, 1 - slot, kind)
                far_weights(g, b, slot, kind, True)

    @pl.when(lin == 0)
    def _():
        far_pass(0)

    @pl.when(lin == 1)
    def _():
        far_pass(1)

    @pl.when(lin >= 2)
    def _():
        far_pass(2)

    lane = lax.broadcasted_iota(jnp.int32, (8, 128), 1)
    mine = jnp.zeros((8, 128), F32)
    for g in range(8):
        for e in range(2):
            for p in range(4):
                part = jnp.sum(sh[g, e, :, p * 128 : p * 128 + 128], axis=1, keepdims=True)
                mine = jnp.where(lane == g * 8 + 2 * p + e, part, mine)
    one[xy] = mine
    for step in range(1, 16):
        remote(one.at[xy], one.at[xy], s5, r5, plane(step)).start()

    @pl.loop(EARLY, EARLY + LATE // 2)
    def _(g):
        for b in range(4):
            late_values(g, b)

    store(1)
    many = one.at[pl.ds(0, 15)]
    remote(many, many, s5, r5, me).wait_recv()
    two[zc] = jnp.sum(one[...], axis=0)
    for step in range(1, 16):
        remote(two.at[zc], two.at[zc], s6, r6, column(step)).start()

    @pl.loop(EARLY + LATE // 2, 8)
    def _(g):
        for b in range(4):
            late_values(g, b)

    store(2)
    lots = two.at[pl.ds(0, 15)]
    remote(lots, lots, s6, r6, me).wait_recv()
    total_ref[...] = jnp.sum(two[...], axis=0) * (1.0 / 131072)

    remote(many, many, s5, r5, me).wait_send()
    remote(lots, lots, s6, r6, me).wait_send()
    for h in range(2):
        to_sibling[h].wait_send()
        remote(fifteen[h], fifteen[h], s3.at[h], r3.at[h], me).wait_send()

        @pl.when(relay)
        def _():
            seven = kv.at[c, pl.ds(0, 7 * PIECE), cols[h]]
            remote(seven, seven, s2.at[h], r2.at[h], me).wait_send()

        @pl.when(first)
        def _():
            sent = kv.at[:, pl.ds(0, 496), cols[h]]
            remote(sent, sent, s1.at[h], r1.at[h], me).wait_send()

    for copy in stores:
        copy.wait()

    @pl.when(lin < 255)
    def _():
        for i, ref in enumerate((kx, vx)):
            remote(ref.at[pl.ds(512, WINDOW)], ref.at[pl.ds(0, WINDOW)], se.at[i], re.at[i], me).wait_send()


def finish_kernel(a_ref, t_ref, o_ref, share_ref, buf, come, go):
    parts = [pl.ds(i * 64, 64) for i in range(8)]
    loads = [pltpu.make_async_copy(a_ref.at[part], buf.at[part], come.at[i]) for i, part in enumerate(parts)]
    stores = [pltpu.make_async_copy(buf.at[part], o_ref.at[part], go.at[i]) for i, part in enumerate(parts)]
    for copy in loads:
        copy.start()
    share_ref[...] = t_ref[0, 0:64]
    for load, store in zip(loads, stores):
        load.wait()
        store.start()
    for copy in stores:
        copy.wait()


def local(queries, keys, values, sink_logits):
    vmem = pl.BlockSpec(memory_space=pltpu.VMEM)
    hbm = pl.BlockSpec(memory_space=pl.ANY)
    dma = pltpu.SemaphoreType.DMA
    attended, total = pl.pallas_call(
        kernel,
        in_specs=[pl.BlockSpec(memory_space=pltpu.SMEM), hbm, hbm, hbm],
        out_specs=[hbm, vmem],
        out_shape=[jax.ShapeDtypeStruct((512, 4096), BF16), jax.ShapeDtypeStruct((8, 128), F32)],
        scratch_shapes=[
            pltpu.VMEM((512, 4096), BF16),
            pltpu.VMEM((512, 4096), BF16),
            pltpu.VMEM((640, 512), BF16),
            pltpu.VMEM((640, 512), BF16),
            pltpu.VMEM((2, 512, 512), BF16),
            pltpu.VMEM((8, 2, 640, 256), BF16),
            pltpu.VMEM((8, 2, 512, 256), BF16),
            pltpu.VMEM((8, 80, 640), BF16),
            pltpu.VMEM((8, 80, 512), BF16),
            pltpu.VMEM((8, 4, 2, 64, 512), F32),
            pltpu.VMEM((8, 4, 2, 8, 512), F32),
            pltpu.VMEM((8, 4, 2, 8, 512), F32),
            pltpu.VMEM((2, 2, 512, 512), F32),
            pltpu.VMEM((2, 2, 8, 512), F32),
            pltpu.VMEM((2, 2, 512, 512), BF16),
            pltpu.VMEM((2, 2, 2, 8, 512), F32),
            pltpu.VMEM((LATE * 4, 2, 512, 512), BF16),
            pltpu.VMEM((LATE * 4, 2, 2, 8, 512), F32),
            pltpu.VMEM((9, 2, 8, 512), F32),
            pltpu.VMEM((16, 8, 128), F32),
            pltpu.VMEM((16, 8, 128), F32),
            pltpu.SemaphoreType.REGULAR,
            dma(()),
            dma((2,)),
            dma((3,)),
        ]
        + [dma((2,))] * 8
        + [dma((2,))] * 2
        + [dma(())] * 4,
        compiler_params=pltpu.CompilerParams(
            collective_id=0, has_side_effects=True, vmem_limit_bytes=60 << 20
        ),
    )(sink_logits, queries, keys, values)
    return pl.pallas_call(
        finish_kernel,
        in_specs=[hbm, vmem],
        out_specs=[hbm, vmem],
        out_shape=[jax.ShapeDtypeStruct((512, 4096), BF16), jax.ShapeDtypeStruct((64,), F32)],
        scratch_shapes=[pltpu.VMEM((512, 4096), BF16), dma((8,)), dma((8,))],
    )(attended, total)


def solution(mesh):
    torus = Mesh(mesh.devices.reshape(SIZES), AXES)
    rows = P(AXES, None)
    return jax.shard_map(
        local, mesh=torus, in_specs=(rows, rows, rows, P()), out_specs=(rows, P()), check_vma=False
    )
```

```python
import functools

import jax
import jax.numpy as jnp
from jax import lax
from jax.experimental import pallas as pl
from jax.experimental.pallas import tpu as pltpu
from jax.sharding import Mesh
from jax.sharding import PartitionSpec as P

WINDOW = 128
SINK_TOK = 512
AXES = ("seq_0", "seq_1", "seq_2", "seq_3")
SIZES = (8, 4, 4, 2)
MESH = pl.DeviceIdType.MESH
F32 = jnp.float32
BF16 = jnp.bfloat16
NEG = -1e30
LOG2E = 1.4426950408889634
PIECE = 32
LATE = 4
EARLY = 8 - LATE
NT = (((1,), (1,)), ((), ()))


def signal(sem, device):
    pl.semaphore_signal(sem, inc=1, device_id=device, device_id_type=MESH)


def coords(lin):
    return (lin // 32, lax.rem(lin // 8, 4), lax.rem(lin // 2, 4), lax.rem(lin, 2))


def padded_keys(tile):
    low = lax.broadcasted_iota(jnp.int32, tile.shape, 1) < 64
    wide = tile.astype(F32) * (LOG2E / 8.0)
    high_term = wide.astype(BF16).astype(F32)
    low_term = wide - high_term
    out = []
    for half in range(2):
        here, moved = [], []
        for term in (high_term, low_term):
            alone = jnp.where(low, term, 0.0) if half == 0 else jnp.where(low, 0.0, term)
            here.append(alone.astype(BF16))
            moved.append(pltpu.roll(alone, 64, 1).astype(BF16))
        here = jnp.concatenate(here, axis=1)
        moved = jnp.concatenate(moved, axis=1)
        out.append((here, moved) if half == 0 else (moved, here))
    return out


def fold(x, op):
    parts = [x[i : i + 8] for i in range(0, x.shape[0], 8)]
    while len(parts) > 1:
        odd = parts[len(parts) // 2 * 2 :]
        parts = [op(parts[i], parts[i + 1]) for i in range(0, len(parts) - 1, 2)] + odd
    return parts[0]


def across(x, op):
    for shift in (4, 2, 1):
        x = op(x, pltpu.roll(x, shift, 0))
    return x


def tall(x, n):
    return jnp.concatenate([x] * n, axis=0)


def kernel(
    sink_ref, q_hbm, k_hbm, v_hbm, o_hbm, total_ref,
    qb, ob, kx, vx, kv, kpw, kps, vtw, vts, ow, mw, lw, sb, tb, pb, rb, late_p, late_r, sh, one, two,
    extra, sq, sk, so, r0, s1, r1, s2, r2, s3, r3, s4, r4, se, re, s5, r5, s6, r6,
):
    z, x, y, c = (lax.axis_index(a) for a in AXES)
    lin = ((z * 4 + x) * 4 + y) * 2 + c
    xy = 4 * x + y
    zc = 2 * z + c
    first = lin == 0
    relay = z == 0
    me = (z, x, y, c)
    rows = pl.ds(pl.multiple_of(xy * PIECE, PIECE), PIECE)
    cols = (pl.ds(0, 256), pl.ds(256, 256))

    def plane(step):
        return (z, lax.rem(x + step // 4, 4), lax.rem(y + step % 4, 4), c)

    def column(step):
        at = lax.rem(zc + step, 16)
        return (at // 2, x, y, lax.rem(at, 2))

    def remote(src, dst, send, recv, device):
        return pltpu.make_async_remote_copy(
            src_ref=src, dst_ref=dst, send_sem=send, recv_sem=recv, device_id=device, device_id_type=MESH
        )

    loads = [
        pltpu.make_async_copy(k_hbm, kx.at[pl.ds(WINDOW, 512)], sk.at[0]),
        pltpu.make_async_copy(v_hbm, vx.at[pl.ds(WINDOW, 512)], sk.at[1]),
    ]
    q_load = pltpu.make_async_copy(q_hbm, qb, sq)
    for copy in loads:
        copy.start()
    q_load.start()

    barrier = pltpu.get_barrier_semaphore()

    @pl.when(relay & (c == 1))
    def _():
        signal(barrier, (0, 0, 0, 0))

    for step in range(1, 16):
        signal(barrier, plane(step))
    signal(barrier, (z, x, y, 1 - c))

    @pl.when((c == 0) & (lin > 0))
    def _():
        signal(barrier, coords(lin - 1))

    corner = (x == 0) & (y == 0)

    @pl.when((z > 0) & corner)
    def _():
        signal(barrier, (0, 0, 0, 1))

    @pl.when((z > 0) & jnp.logical_not(corner))
    def _():
        signal(barrier, (0, x, y, c))

    helper = lin == 1
    from_next = jnp.where((c == 1) & (lin < 255), 1, 0)
    from_column = jnp.where(relay & (lin > 1), 7, 0) + jnp.where(helper, 14, 0)
    pl.semaphore_wait(barrier, 16 + from_next + jnp.where(first, 16, 0) + from_column)

    for copy in loads:
        copy.wait()

    @pl.when(first)
    def _():
        for h in range(2):
            for p in range(16):
                for cc, ref in ((0, kx), (1, vx)):
                    src = ref.at[pl.ds(WINDOW + p * PIECE, PIECE), cols[h]]
                    dst = kv.at[cc, pl.ds(p * PIECE, PIECE), cols[h]]
                    if cc == 0 and p == 0:
                        pltpu.make_async_copy(src, dst, r1.at[h]).start()
                        remote(src, extra.at[:, cols[h]], s1.at[h], r0.at[h], (0, 0, 0, 1)).start()
                    else:
                        remote(src, dst, s1.at[h], r1.at[h], (0, p // 4, p % 4, cc)).start()
        for i, ref in enumerate((kx, vx)):
            ref[pl.ds(0, WINDOW), :] = jnp.zeros((WINDOW, 512), BF16)

    @pl.when(lin < 255)
    def _():
        for i, ref in enumerate((kx, vx)):
            remote(ref.at[pl.ds(512, WINDOW)], ref.at[pl.ds(0, WINDOW)], se.at[i], re.at[i], coords(lin + 1)).start()

    def prepare(kp, vt, keys, values, start, size, src, pairs=range(4)):
        for pair in pairs:
            lanes = pl.ds(pair * 128, 128)
            made = padded_keys(keys[pl.ds(src, size), lanes])
            turned = values[pl.ds(src, size), lanes].T.reshape(2, 64, size)
            for half in range(2):
                g = 2 * pair + half
                for e in range(2):
                    kp[g, e, start : start + size, :] = made[half][e]
                vt[g, 0:64, start : start + size] = turned[half]

    vtw[:, 64:80, :] = jnp.ones((8, 16, 640), BF16)
    vts[:, 64:80, :] = jnp.ones((8, 16, 512), BF16)
    prepare(kpw, vtw, kx, vx, WINDOW, 512, WINDOW)

    row = lax.broadcasted_iota(jnp.int32, (128, 512), 0)
    col = lax.rem(lax.broadcasted_iota(jnp.int32, (128, 512), 1), 128)
    own = row <= col
    which = lax.broadcasted_iota(jnp.int32, (8, 512), 1) // 128

    def q_tile(g, b):
        cols = [
            qb[b * 128 : b * 128 + 128, pl.ds(pl.multiple_of(g * 512 + p * 128, 128), 128)] for p in range(4)
        ]
        tile = jnp.concatenate(cols, axis=0)
        return jnp.concatenate([tile, tile], axis=1)

    def sink_row(g, e):
        out = jnp.full((8, 512), sink_ref[g * 8 + e] * LOG2E, F32)
        for p in range(1, 4):
            out = jnp.where(which == p, sink_ref[g * 8 + 2 * p + e] * LOG2E, out)
        return out

    def near_scores(g, b, slot):
        start = b * 128
        both = jnp.concatenate([kpw[g, e, start : start + 256, :] for e in range(2)], axis=0)
        s = lax.dot_general(both, q_tile(g, b), NT, preferred_element_type=F32)
        for e in range(2):
            before = s[e * 256 : e * 256 + 128]
            if b == 0:
                before = jnp.where(first, NEG, before)
            w = jnp.where(own, s[e * 256 + 128 : e * 256 + 256], before)
            sb[slot, e, :128] = w
            tb[slot, e] = fold(w, jnp.maximum)

    def near_weights(g, b, slot):
        for e in range(2):
            sink = sink_row(g, e)
            top = jnp.maximum(across(tb[slot, e], jnp.maximum), sink)
            w = jnp.exp2(sb[slot, e, :128] - tall(top, 16))
            pb[slot, e, :128] = jnp.where(own, 0.0, w).astype(BF16)
            pb[slot, e, 128:256] = jnp.where(own, w, 0.0).astype(BF16)
            mw[g, b, e] = top
            rb[slot, e, 0] = jnp.exp2(sink - top)

    def near_values(g, b, slot):
        for e in range(2):
            o = jnp.dot(vtw[g, :, b * 128 : b * 128 + 256], pb[slot, e, :256], preferred_element_type=F32)
            ow[g, b, e] = o[:64]
            lw[g, b, e] = rb[slot, e, 0] + o[64:72]

    def near_pass(blocks):
        units = [(h, b) for h in range(2) for b in blocks]
        n = len(units)
        near_scores(0, blocks[0], 0)

        @pl.loop(0, 4)
        def _(pair):
            for u, (h, b) in enumerate(units):
                slot = u % 2
                if u + 1 < n:
                    near_scores(2 * pair + units[u + 1][0], units[u + 1][1], 1 - slot)
                else:
                    near_scores(jnp.minimum(2 * pair + 2, 6), blocks[0], 1 - slot)
                if u > 0:
                    near_values(2 * pair + units[u - 1][0], units[u - 1][1], 1 - slot)
                else:
                    near_values(jnp.maximum(2 * pair - 1, 0), units[n - 1][1], 1 - slot)
                near_weights(2 * pair + h, b, slot)

        near_values(7, blocks[-1], 1)

    piece = [kv.at[c, rows, cols[h]] for h in range(2)]

    def spread_plane(h):
        for step in range(1, 16):
            remote(piece[h], piece[h], s3.at[h], r3.at[h], plane(step)).start()

    q_load.wait()
    pb[...] = jnp.zeros_like(pb)
    rb[...] = jnp.zeros_like(rb)

    @pl.when(relay)
    def _():
        for h in range(2):
            remote(piece[h], piece[h], s2.at[h], r1.at[h], me).wait_recv()

            @pl.when(lin > 0)
            def _():
                for zz in range(1, 8):
                    remote(piece[h], piece[h], s2.at[h], r2.at[h], (zz, x, y, c)).start()

            @pl.when(helper)
            def _():
                spare = extra.at[:, cols[h]]
                remote(spare, spare, s2.at[h], r0.at[h], me).wait_recv()
                for zz in range(1, 8):
                    target = kv.at[0, pl.ds(0, PIECE), cols[h]]
                    remote(spare, target, s2.at[h], r2.at[h], (zz, 0, 0, 0)).start()

            spread_plane(h)

    near_pass((3,))

    @pl.when(z > 0)
    def _():
        for h in range(2):
            remote(piece[h], piece[h], s2.at[h], r2.at[h], me).wait_recv()
            spread_plane(h)

    near_pass((2, 1))

    @pl.when(lin > 0)
    def _():
        for i, ref in enumerate((kx, vx)):
            remote(ref.at[pl.ds(512, WINDOW)], ref.at[pl.ds(0, WINDOW)], se.at[i], re.at[i], me).wait_recv()

    prepare(kpw, vtw, kx, vx, 0, WINDOW, 0)

    fifteen = [kv.at[c, pl.ds(0, 15 * PIECE), cols[h]] for h in range(2)]
    to_sibling = [
        remote(kv.at[c, :, cols[h]], kv.at[c, :, cols[h]], s4.at[h], r4.at[h], (z, x, y, 1 - c)) for h in range(2)
    ]

    def gathered(h):
        remote(fifteen[h], fifteen[h], s3.at[h], r3.at[h], me).wait_recv()
        to_sibling[h].start()

    def arrived(h):
        to_sibling[h].wait_recv()
        prepare(kps, vts, kv.at[0], kv.at[1], 0, 512, 0, (2 * h, 2 * h + 1))

    gathered(0)
    near_pass((0,))
    arrived(0)

    def seen(b, kind):
        if kind == 0:
            return b, b > 0
        return 4, kind == 1 and b == 0

    def far_scores(g, b, slot, kind):
        tiles, diagonal = seen(b, kind)
        if tiles == 0:
            return
        n = tiles * 128
        both = jnp.concatenate([kps[g, e, :n] for e in range(2)], axis=0)
        s = lax.dot_general(both, q_tile(g, b), NT, preferred_element_type=F32)
        for e in range(2):
            part = s[e * n : e * n + n]
            if diagonal:
                last = jnp.where(own, part[n - 128 :], NEG)
                part = last if tiles == 1 else jnp.concatenate([part[: n - 128], last], axis=0)
            sb[slot, e, :n] = part
            tb[slot, e] = fold(part, jnp.maximum)

    def far_weights(g, b, slot, kind, late):
        tiles, _ = seen(b, kind)
        n = tiles * 128
        for e in range(2):
            old = mw[g, b, e]
            top = jnp.maximum(across(tb[slot, e], jnp.maximum), old) if tiles else old
            scale = jnp.exp2(old - top)
            sink = jnp.exp2(sink_row(g, e) - top)
            dst = late_p.at[(g - EARLY) * 4 + b, e] if late else pb.at[slot, e]
            acc = jnp.zeros((8, 512), F32)
            for r in range(0, n, 64):
                w = jnp.exp2(sb[slot, e, r : r + 64] - tall(top, 8))
                dst[r : r + 64, :] = w.astype(BF16)
                if late:
                    acc = acc + fold(w, jnp.add)
            if late:
                if n < 512:
                    dst[n:512, :] = jnp.zeros((512 - n, 512), BF16)
                inverse = 1.0 / (lw[g, b, e] * scale + across(acc, jnp.add))
                sh[g, e] += sink * inverse
                late_r[(g - EARLY) * 4 + b, e, 0] = scale * inverse
                late_r[(g - EARLY) * 4 + b, e, 1] = inverse
            else:
                rb[slot, e, 0] = scale
                rb[slot, e, 1] = sink

    def put(g, b, outs):
        both = jnp.concatenate(outs, axis=0)
        for p in range(4):
            lanes = pl.ds(pl.multiple_of(g * 512 + p * 128, 128), 128)
            ob[b * 128 : b * 128 + 128, lanes] = both[:, p * 128 : p * 128 + 128].T

    def far_values(g, b, slot, share_at, kind):
        outs = []
        n = seen(b, kind)[0] * 128
        for e in range(2):
            if n:
                o = jnp.dot(vts[g, :, :n], pb[slot, e, :n], preferred_element_type=F32)
            else:
                o = jnp.zeros((80, 512), F32)
            scale = rb[slot, e, 0]
            inverse = 1.0 / (lw[g, b, e] * scale + o[64:72])
            sh[share_at, e] += rb[slot, e, 1] * inverse
            outs.append((o[:64] * tall(inverse, 8) + ow[g, b, e] * tall(scale * inverse, 8)).astype(BF16))
        put(g, b, outs)

    def late_values(g, b):
        outs = []
        at = (g - EARLY) * 4 + b
        for e in range(2):
            o = jnp.dot(vts[g, 0:64, :], late_p[at, e], preferred_element_type=F32)
            outs.append((o * tall(late_r[at, e, 1], 8) + ow[g, b, e] * tall(late_r[at, e, 0], 8)).astype(BF16))
        put(g, b, outs)

    sh[...] = jnp.zeros_like(sh)
    spans = (pl.ds(0, 2048), pl.ds(2048, 1024), pl.ds(3072, 1024))
    stores = [pltpu.make_async_copy(ob.at[:, spans[i]], o_hbm.at[:, spans[i]], so.at[i]) for i in range(3)]

    def store(i):
        stores[i].start()


    def far_pass(kind):
        far_scores(0, 0, 0, kind)

        @pl.loop(0, EARLY)
        def _(g):
            @pl.when(g == 1)
            def _():
                gathered(1)

            for b in range(4):
                slot = b % 2
                if b < 3:
                    far_scores(g, b + 1, 1 - slot, kind)
                else:
                    far_scores(jnp.minimum(g + 1, EARLY - 1), 0, 1 - slot, kind)
                if b > 0:
                    far_values(g, b - 1, 1 - slot, g, kind)
                else:
                    far_values(jnp.maximum(g - 1, 0), 3, 1 - slot, jnp.where(g > 0, g - 1, 8), kind)
                far_weights(g, b, slot, kind, False)

        far_values(EARLY - 1, 3, 1, EARLY - 1, kind)
        store(0)
        arrived(1)
        far_scores(EARLY, 0, 0, kind)

        @pl.loop(EARLY, 8)
        def _(g):
            for b in range(4):
                slot = b % 2
                if b < 3:
                    far_scores(g, b + 1, 1 - slot, kind)
                else:
                    far_scores(jnp.minimum(g + 1, 7), 0, 1 - slot, kind)
                far_weights(g, b, slot, kind, True)

    @pl.when(lin == 0)
    def _():
        far_pass(0)

    @pl.when(lin == 1)
    def _():
        far_pass(1)

    @pl.when(lin >= 2)
    def _():
        far_pass(2)

    lane = lax.broadcasted_iota(jnp.int32, (8, 128), 1)
    mine = jnp.zeros((8, 128), F32)
    for g in range(8):
        for e in range(2):
            for p in range(4):
                part = jnp.sum(sh[g, e, :, p * 128 : p * 128 + 128], axis=1, keepdims=True)
                mine = jnp.where(lane == g * 8 + 2 * p + e, part, mine)
    one[xy] = mine
    for step in range(1, 16):
        remote(one.at[xy], one.at[xy], s5, r5, plane(step)).start()

    @pl.loop(EARLY, EARLY + LATE // 2)
    def _(g):
        for b in range(4):
            late_values(g, b)

    store(1)
    many = one.at[pl.ds(0, 15)]
    remote(many, many, s5, r5, me).wait_recv()
    two[zc] = jnp.sum(one[...], axis=0)
    for step in range(1, 16):
        remote(two.at[zc], two.at[zc], s6, r6, column(step)).start()

    @pl.loop(EARLY + LATE // 2, 8)
    def _(g):
        for b in range(4):
            late_values(g, b)

    store(2)
    lots = two.at[pl.ds(0, 15)]
    remote(lots, lots, s6, r6, me).wait_recv()
    total_ref[...] = jnp.sum(two[...], axis=0) * (1.0 / 131072)

    remote(many, many, s5, r5, me).wait_send()
    remote(lots, lots, s6, r6, me).wait_send()
    for h in range(2):
        to_sibling[h].wait_send()
        remote(fifteen[h], fifteen[h], s3.at[h], r3.at[h], me).wait_send()

        @pl.when(helper)
        def _():
            twice = kv.at[c, pl.ds(0, 14 * PIECE), cols[h]]
            remote(twice, twice, s2.at[h], r2.at[h], me).wait_send()

        @pl.when(relay & (lin > 1))
        def _():
            seven = kv.at[c, pl.ds(0, 7 * PIECE), cols[h]]
            remote(seven, seven, s2.at[h], r2.at[h], me).wait_send()

        @pl.when(first)
        def _():
            sent = kv.at[:, :, cols[h]]
            remote(sent, sent, s1.at[h], r1.at[h], me).wait_send()

    for copy in stores:
        copy.wait()

    @pl.when(lin < 255)
    def _():
        for i, ref in enumerate((kx, vx)):
            remote(ref.at[pl.ds(512, WINDOW)], ref.at[pl.ds(0, WINDOW)], se.at[i], re.at[i], me).wait_send()


def finish_kernel(a_ref, t_ref, o_ref, share_ref, buf, come, go):
    parts = [pl.ds(i * 64, 64) for i in range(8)]
    loads = [pltpu.make_async_copy(a_ref.at[part], buf.at[part], come.at[i]) for i, part in enumerate(parts)]
    stores = [pltpu.make_async_copy(buf.at[part], o_ref.at[part], go.at[i]) for i, part in enumerate(parts)]
    for copy in loads:
        copy.start()
    share_ref[...] = t_ref[0, 0:64]
    for load, store in zip(loads, stores):
        load.wait()
        store.start()
    for copy in stores:
        copy.wait()


def local(queries, keys, values, sink_logits):
    vmem = pl.BlockSpec(memory_space=pltpu.VMEM)
    hbm = pl.BlockSpec(memory_space=pl.ANY)
    dma = pltpu.SemaphoreType.DMA
    attended, total = pl.pallas_call(
        kernel,
        in_specs=[pl.BlockSpec(memory_space=pltpu.SMEM), hbm, hbm, hbm],
        out_specs=[hbm, vmem],
        out_shape=[jax.ShapeDtypeStruct((512, 4096), BF16), jax.ShapeDtypeStruct((8, 128), F32)],
        scratch_shapes=[
            pltpu.VMEM((512, 4096), BF16),
            pltpu.VMEM((512, 4096), BF16),
            pltpu.VMEM((640, 512), BF16),
            pltpu.VMEM((640, 512), BF16),
            pltpu.VMEM((2, 512, 512), BF16),
            pltpu.VMEM((8, 2, 640, 256), BF16),
            pltpu.VMEM((8, 2, 512, 256), BF16),
            pltpu.VMEM((8, 80, 640), BF16),
            pltpu.VMEM((8, 80, 512), BF16),
            pltpu.VMEM((8, 4, 2, 64, 512), F32),
            pltpu.VMEM((8, 4, 2, 8, 512), F32),
            pltpu.VMEM((8, 4, 2, 8, 512), F32),
            pltpu.VMEM((2, 2, 512, 512), F32),
            pltpu.VMEM((2, 2, 8, 512), F32),
            pltpu.VMEM((2, 2, 512, 512), BF16),
            pltpu.VMEM((2, 2, 2, 8, 512), F32),
            pltpu.VMEM((LATE * 4, 2, 512, 512), BF16),
            pltpu.VMEM((LATE * 4, 2, 2, 8, 512), F32),
            pltpu.VMEM((9, 2, 8, 512), F32),
            pltpu.VMEM((16, 8, 128), F32),
            pltpu.VMEM((16, 8, 128), F32),
            pltpu.VMEM((PIECE, 512), BF16),
            dma(()),
            dma((2,)),
            dma((3,)),
            dma((2,)),
        ]
        + [dma((2,))] * 8
        + [dma((2,))] * 2
        + [dma(())] * 4,
        compiler_params=pltpu.CompilerParams(
            collective_id=0, has_side_effects=True, vmem_limit_bytes=60 << 20
        ),
    )(sink_logits, queries, keys, values)
    return pl.pallas_call(
        finish_kernel,
        in_specs=[hbm, vmem],
        out_specs=[hbm, vmem],
        out_shape=[jax.ShapeDtypeStruct((512, 4096), BF16), jax.ShapeDtypeStruct((64,), F32)],
        scratch_shapes=[pltpu.VMEM((512, 4096), BF16), dma((8,)), dma((8,))],
    )(attended, total)


def solution(mesh):
    torus = Mesh(mesh.devices.reshape(SIZES), AXES)
    rows = P(AXES, None)
    return jax.shard_map(
        local, mesh=torus, in_specs=(rows, rows, rows, P()), out_specs=(rows, P()), check_vma=False
    )
```

```python
import functools

import jax
import jax.numpy as jnp
from jax import lax
from jax.experimental import pallas as pl
from jax.experimental.pallas import tpu as pltpu
from jax.sharding import Mesh
from jax.sharding import PartitionSpec as P

WINDOW = 128
SINK_TOK = 512
AXES = ("seq_0", "seq_1", "seq_2", "seq_3")
SIZES = (8, 4, 4, 2)
MESH = pl.DeviceIdType.MESH
F32 = jnp.float32
BF16 = jnp.bfloat16
NEG = -1e30
LOG2E = 1.4426950408889634
PIECE = 32
LATE = 4
EARLY = 8 - LATE
NT = (((1,), (1,)), ((), ()))


def signal(sem, device):
    pl.semaphore_signal(sem, inc=1, device_id=device, device_id_type=MESH)


def coords(lin):
    return (lin // 32, lax.rem(lin // 8, 4), lax.rem(lin // 2, 4), lax.rem(lin, 2))


def padded_keys(tile):
    low = lax.broadcasted_iota(jnp.int32, tile.shape, 1) < 64
    wide = tile.astype(F32) * (LOG2E / 8.0)
    high_term = wide.astype(BF16).astype(F32)
    low_term = wide - high_term
    out = []
    for half in range(2):
        here, moved = [], []
        for term in (high_term, low_term):
            alone = jnp.where(low, term, 0.0) if half == 0 else jnp.where(low, 0.0, term)
            here.append(alone.astype(BF16))
            moved.append(pltpu.roll(alone, 64, 1).astype(BF16))
        here = jnp.concatenate(here, axis=1)
        moved = jnp.concatenate(moved, axis=1)
        out.append((here, moved) if half == 0 else (moved, here))
    return out


def fold(x, op):
    parts = [x[i : i + 8] for i in range(0, x.shape[0], 8)]
    while len(parts) > 1:
        odd = parts[len(parts) // 2 * 2 :]
        parts = [op(parts[i], parts[i + 1]) for i in range(0, len(parts) - 1, 2)] + odd
    return parts[0]


def across(x, op):
    for shift in (4, 2, 1):
        x = op(x, pltpu.roll(x, shift, 0))
    return x


def tall(x, n):
    return jnp.concatenate([x] * n, axis=0)


def kernel(
    sink_ref, q_hbm, k_hbm, v_hbm, o_hbm, total_ref,
    qb, ob, kx, vx, kv, kpw, kps, vtw, vts, ow, mw, lw, sb, tb, pb, rb, late_p, late_r, sh, one, two,
    ready, sq, sk, so, s1, r1, s2, r2, s3, r3, s4, r4, se, re, s5, r5, s6, r6,
):
    z, x, y, c = (lax.axis_index(a) for a in AXES)
    lin = ((z * 4 + x) * 4 + y) * 2 + c
    xy = 4 * x + y
    zc = 2 * z + c
    first = lin == 0
    relay = z == 0
    me = (z, x, y, c)
    rows = pl.ds(pl.multiple_of(xy * PIECE, PIECE), PIECE)
    cols = (pl.ds(0, 256), pl.ds(256, 256))

    def plane(step):
        return (z, lax.rem(x + step // 4, 4), lax.rem(y + step % 4, 4), c)

    def column(step):
        at = lax.rem(zc + step, 16)
        return (at // 2, x, y, lax.rem(at, 2))

    def remote(src, dst, send, recv, device):
        return pltpu.make_async_remote_copy(
            src_ref=src, dst_ref=dst, send_sem=send, recv_sem=recv, device_id=device, device_id_type=MESH
        )

    loads = [
        pltpu.make_async_copy(k_hbm, kx.at[pl.ds(WINDOW, 512)], sk.at[0]),
        pltpu.make_async_copy(v_hbm, vx.at[pl.ds(WINDOW, 512)], sk.at[1]),
    ]
    q_load = pltpu.make_async_copy(q_hbm, qb, sq)
    for copy in loads:
        copy.start()
    q_load.start()

    barrier = pltpu.get_barrier_semaphore()

    @pl.when(relay & (c == 1))
    def _():
        signal(barrier, (0, 0, 0, 0))

    for step in range(1, 16):
        signal(barrier, plane(step))
    signal(barrier, (z, x, y, 1 - c))

    @pl.when((c == 0) & (lin > 0))
    def _():
        signal(barrier, coords(lin - 1))

    @pl.when(relay)
    def _():
        for zz in range(1, 8):
            signal(barrier, (zz, x, y, c))

    from_next = jnp.where((c == 1) & (lin < 255), 1, 0)
    pl.semaphore_wait(barrier, 16 + from_next + jnp.where(first, 16, 0) + jnp.where(relay, 0, 1))

    @pl.when(z > 0)
    def _():
        signal(ready, (0, x, y, c))

    for copy in loads:
        copy.wait()

    @pl.when(first)
    def _():
        for h in range(2):
            for p in range(16):
                for cc, ref in ((0, kx), (1, vx)):
                    src = ref.at[pl.ds(WINDOW + p * PIECE, PIECE), cols[h]]
                    dst = kv.at[cc, pl.ds(p * PIECE, PIECE), cols[h]]
                    if cc == 0 and p == 0:
                        pltpu.make_async_copy(src, dst, r1.at[h]).start()
                    else:
                        remote(src, dst, s1.at[h], r1.at[h], (0, p // 4, p % 4, cc)).start()
        for i, ref in enumerate((kx, vx)):
            ref[pl.ds(0, WINDOW), :] = jnp.zeros((WINDOW, 512), BF16)

    @pl.when(lin < 255)
    def _():
        for i, ref in enumerate((kx, vx)):
            remote(ref.at[pl.ds(512, WINDOW)], ref.at[pl.ds(0, WINDOW)], se.at[i], re.at[i], coords(lin + 1)).start()

    def prepare(kp, vt, keys, values, start, size, src, pairs=range(4)):
        for pair in pairs:
            lanes = pl.ds(pair * 128, 128)
            made = padded_keys(keys[pl.ds(src, size), lanes])
            turned = values[pl.ds(src, size), lanes].T.reshape(2, 64, size)
            for half in range(2):
                g = 2 * pair + half
                for e in range(2):
                    kp[g, e, start : start + size, :] = made[half][e]
                vt[g, 0:64, start : start + size] = turned[half]

    vtw[:, 64:80, :] = jnp.ones((8, 16, 640), BF16)
    vts[:, 64:80, :] = jnp.ones((8, 16, 512), BF16)
    prepare(kpw, vtw, kx, vx, WINDOW, 512, WINDOW)

    row = lax.broadcasted_iota(jnp.int32, (128, 512), 0)
    col = lax.rem(lax.broadcasted_iota(jnp.int32, (128, 512), 1), 128)
    own = row <= col
    which = lax.broadcasted_iota(jnp.int32, (8, 512), 1) // 128

    def q_tile(g, b):
        cols = [
            qb[b * 128 : b * 128 + 128, pl.ds(pl.multiple_of(g * 512 + p * 128, 128), 128)] for p in range(4)
        ]
        tile = jnp.concatenate(cols, axis=0)
        return jnp.concatenate([tile, tile], axis=1)

    def sink_row(g, e):
        out = jnp.full((8, 512), sink_ref[g * 8 + e] * LOG2E, F32)
        for p in range(1, 4):
            out = jnp.where(which == p, sink_ref[g * 8 + 2 * p + e] * LOG2E, out)
        return out

    def near_scores(g, b, slot):
        start = b * 128
        both = jnp.concatenate([kpw[g, e, start : start + 256, :] for e in range(2)], axis=0)
        s = lax.dot_general(both, q_tile(g, b), NT, preferred_element_type=F32)
        for e in range(2):
            before = s[e * 256 : e * 256 + 128]
            if b == 0:
                before = jnp.where(first, NEG, before)
            w = jnp.where(own, s[e * 256 + 128 : e * 256 + 256], before)
            sb[slot, e, :128] = w
            tb[slot, e] = fold(w, jnp.maximum)

    def near_weights(g, b, slot):
        for e in range(2):
            sink = sink_row(g, e)
            top = jnp.maximum(across(tb[slot, e], jnp.maximum), sink)
            w = jnp.exp2(sb[slot, e, :128] - tall(top, 16))
            pb[slot, e, :128] = jnp.where(own, 0.0, w).astype(BF16)
            pb[slot, e, 128:256] = jnp.where(own, w, 0.0).astype(BF16)
            mw[g, b, e] = top
            rb[slot, e, 0] = jnp.exp2(sink - top)

    def near_values(g, b, slot):
        for e in range(2):
            o = jnp.dot(vtw[g, :, b * 128 : b * 128 + 256], pb[slot, e, :256], preferred_element_type=F32)
            ow[g, b, e] = o[:64]
            lw[g, b, e] = rb[slot, e, 0] + o[64:72]

    def near_pass(blocks):
        units = [(h, b) for h in range(2) for b in blocks]
        n = len(units)
        near_scores(0, blocks[0], 0)

        @pl.loop(0, 4)
        def _(pair):
            for u, (h, b) in enumerate(units):
                slot = u % 2
                if u + 1 < n:
                    near_scores(2 * pair + units[u + 1][0], units[u + 1][1], 1 - slot)
                else:
                    near_scores(jnp.minimum(2 * pair + 2, 6), blocks[0], 1 - slot)
                if u > 0:
                    near_values(2 * pair + units[u - 1][0], units[u - 1][1], 1 - slot)
                else:
                    near_values(jnp.maximum(2 * pair - 1, 0), units[n - 1][1], 1 - slot)
                near_weights(2 * pair + h, b, slot)

        near_values(7, blocks[-1], 1)

    piece = [kv.at[c, rows, cols[h]] for h in range(2)]

    def spread_plane(h):
        for step in range(1, 16):
            remote(piece[h], piece[h], s3.at[h], r3.at[h], plane(step)).start()

    q_load.wait()
    pb[...] = jnp.zeros_like(pb)
    rb[...] = jnp.zeros_like(rb)
    near_pass((3, 2))

    @pl.when(relay)
    def _():
        pl.semaphore_wait(ready, 7)
        for h in range(2):
            remote(piece[h], piece[h], s2.at[h], r1.at[h], me).wait_recv()
            for zz in range(1, 8):
                remote(piece[h], piece[h], s2.at[h], r2.at[h], (zz, x, y, c)).start()
            if h == 0:
                spread_plane(0)

    near_pass((1,))

    @pl.when(z > 0)
    def _():
        remote(piece[0], piece[0], s2.at[0], r2.at[0], me).wait_recv()
        spread_plane(0)

    @pl.when(lin > 0)
    def _():
        for i, ref in enumerate((kx, vx)):
            remote(ref.at[pl.ds(512, WINDOW)], ref.at[pl.ds(0, WINDOW)], se.at[i], re.at[i], me).wait_recv()

    prepare(kpw, vtw, kx, vx, 0, WINDOW, 0)
    near_pass((0,))

    fifteen = [kv.at[c, pl.ds(0, 15 * PIECE), cols[h]] for h in range(2)]
    to_sibling = [
        remote(kv.at[c, :, cols[h]], kv.at[c, :, cols[h]], s4.at[h], r4.at[h], (z, x, y, 1 - c)) for h in range(2)
    ]

    def gathered(h):
        remote(fifteen[h], fifteen[h], s3.at[h], r3.at[h], me).wait_recv()
        to_sibling[h].start()

    def arrived(h):
        to_sibling[h].wait_recv()
        prepare(kps, vts, kv.at[0], kv.at[1], 0, 512, 0, (2 * h, 2 * h + 1))

    gathered(0)

    @pl.when(z > 0)
    def _():
        remote(piece[1], piece[1], s2.at[1], r2.at[1], me).wait_recv()

    spread_plane(1)
    arrived(0)

    def seen(b, kind):
        if kind == 0:
            return b, b > 0
        return 4, kind == 1 and b == 0

    def far_scores(g, b, slot, kind):
        tiles, diagonal = seen(b, kind)
        if tiles == 0:
            return
        n = tiles * 128
        both = jnp.concatenate([kps[g, e, :n] for e in range(2)], axis=0)
        s = lax.dot_general(both, q_tile(g, b), NT, preferred_element_type=F32)
        for e in range(2):
            part = s[e * n : e * n + n]
            if diagonal:
                last = jnp.where(own, part[n - 128 :], NEG)
                part = last if tiles == 1 else jnp.concatenate([part[: n - 128], last], axis=0)
            sb[slot, e, :n] = part
            tb[slot, e] = fold(part, jnp.maximum)

    def far_weights(g, b, slot, kind, late):
        tiles, _ = seen(b, kind)
        n = tiles * 128
        for e in range(2):
            old = mw[g, b, e]
            top = jnp.maximum(across(tb[slot, e], jnp.maximum), old) if tiles else old
            scale = jnp.exp2(old - top)
            sink = jnp.exp2(sink_row(g, e) - top)
            dst = late_p.at[(g - EARLY) * 4 + b, e] if late else pb.at[slot, e]
            acc = jnp.zeros((8, 512), F32)
            for r in range(0, n, 64):
                w = jnp.exp2(sb[slot, e, r : r + 64] - tall(top, 8))
                dst[r : r + 64, :] = w.astype(BF16)
                if late:
                    acc = acc + fold(w, jnp.add)
            if late:
                if n < 512:
                    dst[n:512, :] = jnp.zeros((512 - n, 512), BF16)
                inverse = 1.0 / (lw[g, b, e] * scale + across(acc, jnp.add))
                sh[g, e] += sink * inverse
                late_r[(g - EARLY) * 4 + b, e, 0] = scale * inverse
                late_r[(g - EARLY) * 4 + b, e, 1] = inverse
            else:
                rb[slot, e, 0] = scale
                rb[slot, e, 1] = sink

    def put(g, b, outs):
        both = jnp.concatenate(outs, axis=0)
        for p in range(4):
            lanes = pl.ds(pl.multiple_of(g * 512 + p * 128, 128), 128)
            ob[b * 128 : b * 128 + 128, lanes] = both[:, p * 128 : p * 128 + 128].T

    def far_values(g, b, slot, share_at, kind):
        outs = []
        n = seen(b, kind)[0] * 128
        for e in range(2):
            if n:
                o = jnp.dot(vts[g, :, :n], pb[slot, e, :n], preferred_element_type=F32)
            else:
                o = jnp.zeros((80, 512), F32)
            scale = rb[slot, e, 0]
            inverse = 1.0 / (lw[g, b, e] * scale + o[64:72])
            sh[share_at, e] += rb[slot, e, 1] * inverse
            outs.append((o[:64] * tall(inverse, 8) + ow[g, b, e] * tall(scale * inverse, 8)).astype(BF16))
        put(g, b, outs)

    def late_values(g, b):
        outs = []
        at = (g - EARLY) * 4 + b
        for e in range(2):
            o = jnp.dot(vts[g, 0:64, :], late_p[at, e], preferred_element_type=F32)
            outs.append((o * tall(late_r[at, e, 1], 8) + ow[g, b, e] * tall(late_r[at, e, 0], 8)).astype(BF16))
        put(g, b, outs)

    sh[...] = jnp.zeros_like(sh)
    spans = (pl.ds(0, 2048), pl.ds(2048, 1024), pl.ds(3072, 1024))
    stores = [pltpu.make_async_copy(ob.at[:, spans[i]], o_hbm.at[:, spans[i]], so.at[i]) for i in range(3)]

    def store(i):
        stores[i].start()


    def far_pass(kind):
        far_scores(0, 0, 0, kind)

        @pl.loop(0, EARLY)
        def _(g):
            @pl.when(g == 1)
            def _():
                gathered(1)

            for b in range(4):
                slot = b % 2
                if b < 3:
                    far_scores(g, b + 1, 1 - slot, kind)
                else:
                    far_scores(jnp.minimum(g + 1, EARLY - 1), 0, 1 - slot, kind)
                if b > 0:
                    far_values(g, b - 1, 1 - slot, g, kind)
                else:
                    far_values(jnp.maximum(g - 1, 0), 3, 1 - slot, jnp.where(g > 0, g - 1, 8), kind)
                far_weights(g, b, slot, kind, False)

        far_values(EARLY - 1, 3, 1, EARLY - 1, kind)
        store(0)
        arrived(1)
        far_scores(EARLY, 0, 0, kind)

        @pl.loop(EARLY, 8)
        def _(g):
            for b in range(4):
                slot = b % 2
                if b < 3:
                    far_scores(g, b + 1, 1 - slot, kind)
                else:
                    far_scores(jnp.minimum(g + 1, 7), 0, 1 - slot, kind)
                far_weights(g, b, slot, kind, True)

    @pl.when(lin == 0)
    def _():
        far_pass(0)

    @pl.when(lin == 1)
    def _():
        far_pass(1)

    @pl.when(lin >= 2)
    def _():
        far_pass(2)

    lane = lax.broadcasted_iota(jnp.int32, (8, 128), 1)
    mine = jnp.zeros((8, 128), F32)
    for g in range(8):
        for e in range(2):
            for p in range(4):
                part = jnp.sum(sh[g, e, :, p * 128 : p * 128 + 128], axis=1, keepdims=True)
                mine = jnp.where(lane == g * 8 + 2 * p + e, part, mine)
    one[xy] = mine
    for step in range(1, 16):
        remote(one.at[xy], one.at[xy], s5, r5, plane(step)).start()

    @pl.loop(EARLY, EARLY + LATE // 2)
    def _(g):
        for b in range(4):
            late_values(g, b)

    store(1)
    many = one.at[pl.ds(0, 15)]
    remote(many, many, s5, r5, me).wait_recv()
    two[zc] = jnp.sum(one[...], axis=0)
    for step in range(1, 16):
        remote(two.at[zc], two.at[zc], s6, r6, column(step)).start()

    @pl.loop(EARLY + LATE // 2, 8)
    def _(g):
        for b in range(4):
            late_values(g, b)

    store(2)
    lots = two.at[pl.ds(0, 15)]
    remote(lots, lots, s6, r6, me).wait_recv()
    total_ref[...] = jnp.sum(two[...], axis=0) * (1.0 / 131072)

    remote(many, many, s5, r5, me).wait_send()
    remote(lots, lots, s6, r6, me).wait_send()
    for h in range(2):
        to_sibling[h].wait_send()
        remote(fifteen[h], fifteen[h], s3.at[h], r3.at[h], me).wait_send()

        @pl.when(relay)
        def _():
            seven = kv.at[c, pl.ds(0, 7 * PIECE), cols[h]]
            remote(seven, seven, s2.at[h], r2.at[h], me).wait_send()

        @pl.when(first)
        def _():
            sent = kv.at[:, pl.ds(0, 496), cols[h]]
            remote(sent, sent, s1.at[h], r1.at[h], me).wait_send()

    for copy in stores:
        copy.wait()

    @pl.when(lin < 255)
    def _():
        for i, ref in enumerate((kx, vx)):
            remote(ref.at[pl.ds(512, WINDOW)], ref.at[pl.ds(0, WINDOW)], se.at[i], re.at[i], me).wait_send()


def finish_kernel(a_ref, t_ref, o_ref, share_ref, buf, come, go):
    parts = [pl.ds(i * 64, 64) for i in range(8)]
    loads = [pltpu.make_async_copy(a_ref.at[part], buf.at[part], come.at[i]) for i, part in enumerate(parts)]
    stores = [pltpu.make_async_copy(buf.at[part], o_ref.at[part], go.at[i]) for i, part in enumerate(parts)]
    for copy in loads:
        copy.start()
    share_ref[...] = t_ref[0, 0:64]
    for load, store in zip(loads, stores):
        load.wait()
        store.start()
    for copy in stores:
        copy.wait()


def local(queries, keys, values, sink_logits):
    vmem = pl.BlockSpec(memory_space=pltpu.VMEM)
    hbm = pl.BlockSpec(memory_space=pl.ANY)
    dma = pltpu.SemaphoreType.DMA
    attended, total = pl.pallas_call(
        kernel,
        in_specs=[pl.BlockSpec(memory_space=pltpu.SMEM), hbm, hbm, hbm],
        out_specs=[hbm, vmem],
        out_shape=[jax.ShapeDtypeStruct((512, 4096), BF16), jax.ShapeDtypeStruct((8, 128), F32)],
        scratch_shapes=[
            pltpu.VMEM((512, 4096), BF16),
            pltpu.VMEM((512, 4096), BF16),
            pltpu.VMEM((640, 512), BF16),
            pltpu.VMEM((640, 512), BF16),
            pltpu.VMEM((2, 512, 512), BF16),
            pltpu.VMEM((8, 2, 640, 256), BF16),
            pltpu.VMEM((8, 2, 512, 256), BF16),
            pltpu.VMEM((8, 80, 640), BF16),
            pltpu.VMEM((8, 80, 512), BF16),
            pltpu.VMEM((8, 4, 2, 64, 512), F32),
            pltpu.VMEM((8, 4, 2, 8, 512), F32),
            pltpu.VMEM((8, 4, 2, 8, 512), F32),
            pltpu.VMEM((2, 2, 512, 512), F32),
            pltpu.VMEM((2, 2, 8, 512), F32),
            pltpu.VMEM((2, 2, 512, 512), BF16),
            pltpu.VMEM((2, 2, 2, 8, 512), F32),
            pltpu.VMEM((LATE * 4, 2, 512, 512), BF16),
            pltpu.VMEM((LATE * 4, 2, 2, 8, 512), F32),
            pltpu.VMEM((9, 2, 8, 512), F32),
            pltpu.VMEM((16, 8, 128), F32),
            pltpu.VMEM((16, 8, 128), F32),
            pltpu.SemaphoreType.REGULAR,
            dma(()),
            dma((2,)),
            dma((3,)),
        ]
        + [dma((2,))] * 8
        + [dma((2,))] * 2
        + [dma(())] * 4,
        compiler_params=pltpu.CompilerParams(
            collective_id=0, has_side_effects=True, vmem_limit_bytes=60 << 20
        ),
    )(sink_logits, queries, keys, values)
    return pl.pallas_call(
        finish_kernel,
        in_specs=[hbm, vmem],
        out_specs=[hbm, vmem],
        out_shape=[jax.ShapeDtypeStruct((512, 4096), BF16), jax.ShapeDtypeStruct((64,), F32)],
        scratch_shapes=[pltpu.VMEM((512, 4096), BF16), dma((8,)), dma((8,))],
    )(attended, total)


def solution(mesh):
    torus = Mesh(mesh.devices.reshape(SIZES), AXES)
    rows = P(AXES, None)
    return jax.shard_map(
        local, mesh=torus, in_specs=(rows, rows, rows, P()), out_specs=(rows, P()), check_vma=False
    )
```
